128 devices in a mesh: gz: 8 (over x, core), xy: 16 (over y, z).
Axes of the slice: x: 4, y: 4, z: 4, core: 2. Of those that a mesh axis runs over, the one named last changes fastest.
Arguments:
- parent_feat: bfloat16 [128, 64, 2048], P(('gz', 'xy')), may hold values from -6 to 6
- parent_cell: int32 [128, 2048], P(('gz', 'xy')), may hold values from 0 to 255
- send_count: int32 [128, 128], P(('gz', 'xy')), may hold values from 1 to 16, as said below
- up_weight: bfloat16 [8, 64, 64], replicated, may hold values from -0.75 to 0.75
- conv_one: bfloat16 [27, 64, 64], replicated, may hold values from -0.15625 to 0.15625
- conv_two: bfloat16 [27, 64, 64], replicated, may hold values from -0.15625 to 0.15625
- child_mask: int32 [32, 8, 1024], P('xy', None, 'gz'), may hold values 0 or 1
- cotangent: bfloat16 [64, 32, 8, 1024], P(None, 'xy', None, 'gz'), may hold values from -6 to 6
Outputs:
- decoded: bfloat16 [64, 32, 8, 1024], P(None, 'xy', None, 'gz')
- grad_parent: bfloat16 [128, 64, 2048], P(('gz', 'xy'))
- grad_one: float32 [27, 64, 64], replicated
- grad_two: float32 [27, 64, 64], replicated
- grad_up: float32 [8, 64, 64], replicated
The draws below stay inside these ranges and needn't reach their ends.
Inputs may be any that keep to these rules, and one draw needn't show every extreme that they name: `send_count`: some receiver gets 16 live slots from every sender, and every sender fills all 16 slots to some receiver. `parent_cell`: several slots may name the same parent voxel; their features add.
All inputs are finite; a program needn't handle non-finite values. No bound on the sum of `child_mask` on one device may be relied on, other than what follows from the above.
Results may differ from the reference program's by a relative error of at most 0.008.
Values may be sent and summed in bfloat16 or wider, within the bound.
No kernel may reach another device: no remote copies, remote signals or barrier semaphores. Data moves between devices by JAX's collectives and lax.ppermute only.
A program may use at most 64 MiB of HBM per device.

```python
import math
import jax
import jax.numpy as jnp
from jax import lax

C = 64
CX = 2
CY = 8
CZ = 128
CAP = 16
XCELLS = 32
ZCELLS = 1024
SLOTS = 2048
PCELLS = 256
N_GZ = 8
N_XY = 16


def draw_send_count(key, part):
    devices_all = SLOTS // CAP
    key_base = jax.random.fold_in(key, 11)
    key_hot = jax.random.fold_in(key, 12)
    key_star = jax.random.fold_in(key, 13)
    base = jax.random.randint(key_base, (devices_all, devices_all), 1, CAP + 1)
    hot = jax.random.randint(key_hot, (devices_all,), 0, devices_all)
    star = jax.random.randint(key_star, (), 0, devices_all)
    target = jnp.arange(devices_all, dtype=jnp.int32)
    full = (target[None, :] == hot[:, None]) | (target[None, :] == star)
    return jnp.where(full, CAP, base).astype(jnp.int32)


def with_ends(array, stream_key, smallest, top_value):
    shape = array.shape
    place = [jax.random.randint(jax.random.fold_in(stream_key, axis), (), 0, shape[axis]) for axis in range(len(shape))]
    array = array.at[tuple(place)].set(smallest)
    longest = shape.index(max(shape))
    place[longest] = (place[longest] + 1) % shape[longest]
    return array.at[tuple(place)].set(top_value)


def steps_of(own_key, extent, cuts, smallest, largest):
    def one(dim, blocks):
        draws = jax.random.uniform(jax.random.fold_in(jax.random.fold_in(own_key, 6), dim), (blocks,), jnp.float32, smallest / len(cuts), largest / len(cuts))
        return jnp.repeat(jnp.exp(draws), extent[dim] // blocks).reshape((-1,) + (1,) * (len(extent) - dim - 1))

    factor_of = one(*cuts[0])
    for cut in cuts[1:]:
        factor_of = factor_of * one(*cut)
    return factor_of


def gaussian(key, dims, scale, limit, pieces=(), held_as=jnp.bfloat16):
    loudness = steps_of(key, dims, pieces, -0.22, 0.18) if pieces else 1.0
    values = jax.random.normal(key, dims, jnp.float32) * scale * loudness
    return jnp.minimum(jnp.maximum(values, -limit), limit).astype(held_as)


def setup_inputs(seed: int = 0) -> dict:
    key_list = jax.random.split(jax.random.key(seed), 9)
    return {
        "parent_feat": gaussian(key_list[0], (N_GZ * N_XY, C, SLOTS), 1.0, 6.0, ((0, 128),)),
        "parent_cell": with_ends(jax.random.randint(key_list[1], (N_GZ * N_XY, SLOTS), 0, PCELLS), jax.random.fold_in(key_list[1], 1), 0, PCELLS - 1).astype(jnp.int32),
        "send_count": draw_send_count(jax.random.fold_in(key_list[8], 71), 0),
        "up_weight": gaussian(key_list[3], (8, C, C), C ** -0.5, 0.75),
        "conv_one": gaussian(key_list[4], (27, C, C), (27 * C) ** -0.5, 0.15625),
        "conv_two": gaussian(key_list[5], (27, C, C), (27 * C) ** -0.5, 0.15625),
        "child_mask": with_ends((jax.random.randint(key_list[6], (XCELLS, CY, ZCELLS), 0, 4) < 3).astype(jnp.int32), jax.random.fold_in(key_list[6], 1), 0, 1),
        "cotangent": gaussian(key_list[7], (C, XCELLS, CY, ZCELLS), 1.0, 6.0, ((1, 16), (3, 8))),
    }


OFFSETS = [(a, b, c) for a in (-1, 0, 1) for b in (-1, 0, 1) for c in (-1, 0, 1)]

def window(padded, offset, direction, shape):
    nx, ny, nz = (shape[1], shape[2], shape[3])
    ox, oy, oz = (offset[0] * direction, offset[1] * direction, offset[2] * direction)
    part = padded[:, 1 + ox:1 + ox + nx, 1 + oy:1 + oy + ny, 1 + oz:1 + oz + nz]
    return part.reshape(shape[0], -1)

def pad_field(field):
    return jnp.pad(field.astype(jnp.float32), ((0, 0), (1, 1), (1, 1), (1, 1)))

def convolve(field, weights, direction):
    padded = pad_field(field)
    total = jnp.zeros((field.shape[0], field.shape[1] * field.shape[2] * field.shape[3]), jnp.float32)
    for index, offset in enumerate(OFFSETS):
        matrix = weights[index].astype(jnp.float32)
        if direction < 0:
            matrix = matrix.T
        total = total + jnp.dot(matrix, window(padded, offset, direction, field.shape), precision=lax.Precision.HIGHEST)
    return total.reshape(field.shape)

def weight_terms(delta, field):
    padded = pad_field(field)
    flat = delta.astype(jnp.float32).reshape(delta.shape[0], -1)
    terms = [jnp.dot(flat, window(padded, offset, 1, field.shape).T, precision=lax.Precision.HIGHEST) for offset in OFFSETS]
    return jnp.stack(terms)

def silu_slope(value):
    sig = jax.nn.sigmoid(value)
    return sig * (1.0 + value * (1.0 - sig))

def to_global(tiles):
    shaped = tiles.reshape(N_GZ, N_XY, C, CX, CY, CZ).transpose(2, 1, 3, 4, 0, 5)
    return shaped.reshape(C, XCELLS, CY, ZCELLS)

def to_tiles(field):
    shaped = field.reshape(C, N_XY, CX, CY, N_GZ, CZ).transpose(4, 1, 0, 2, 3, 5)
    return shaped.reshape(N_GZ * N_XY, C, CX, CY, CZ)

def reference(parent_feat, parent_cell, send_count, up_weight, conv_one, conv_two, child_mask, cotangent):
    devices_all = N_GZ * N_XY
    half_x, half_y, half_z = (CX // 2, CY // 2, CZ // 2)
    slot_pos = jnp.arange(SLOTS, dtype=jnp.int32) % CAP
    live = slot_pos[None, :] < jnp.repeat(send_count, CAP, axis=1)
    feats = jnp.where(live[:, None, :], parent_feat, jnp.zeros_like(parent_feat))
    recv_feat = feats.reshape(devices_all, C, devices_all, CAP).transpose(2, 1, 0, 3).reshape(devices_all, C, SLOTS)
    recv_cell = parent_cell.reshape(devices_all, devices_all, CAP).transpose(1, 0, 2).reshape(devices_all, SLOTS)
    cell_ids = jnp.arange(PCELLS, dtype=jnp.int32)

    def tile_grid(pair):
        feat_block, cell_block = pair
        onehot = (cell_block[:, None] == cell_ids[None, :]).astype(jnp.float32)
        return jnp.dot(feat_block.astype(jnp.float32), onehot, precision=lax.Precision.HIGHEST).astype(jnp.bfloat16)
    grids = lax.map(tile_grid, (recv_feat, recv_cell))
    up8 = jnp.einsum('ocd,ndq->nocq', up_weight.astype(jnp.float32), grids.astype(jnp.float32), precision=lax.Precision.HIGHEST)
    up_tiles = up8.reshape(devices_all, 2, 2, 2, C, half_x, half_y, half_z).transpose(0, 4, 5, 1, 6, 2, 7, 3)
    up = to_global(up_tiles.reshape(devices_all, C, CX, CY, CZ))
    maskf = child_mask.astype(jnp.float32)
    lifted = (maskf * up).astype(jnp.bfloat16)
    first_pre = convolve(lifted, conv_one, 1)
    first_act = (maskf * jax.nn.silu(first_pre)).astype(jnp.bfloat16)
    second_pre = convolve(first_act, conv_two, 1)
    decoded = (maskf * jax.nn.silu(second_pre)).astype(jnp.bfloat16)
    scale = 1.0 / math.sqrt(XCELLS * CY * ZCELLS)
    delta_two = (cotangent.astype(jnp.float32) * maskf * silu_slope(second_pre)).astype(jnp.bfloat16)
    grad_two = weight_terms(delta_two, first_act) * scale
    back_one = convolve(delta_two, conv_two, -1)
    delta_one = (back_one * maskf * silu_slope(first_pre)).astype(jnp.bfloat16)
    grad_one = weight_terms(delta_one, lifted) * scale
    delta_up = (convolve(delta_one, conv_one, -1) * maskf).astype(jnp.bfloat16)
    du_tiles = to_tiles(delta_up).reshape(devices_all, C, half_x, 2, half_y, 2, half_z, 2)
    du8 = du_tiles.transpose(0, 3, 5, 7, 1, 2, 4, 6).reshape(devices_all, 8, C, PCELLS).astype(jnp.float32)
    grad_up = jnp.einsum('nocq,ndq->ocd', du8, grids.astype(jnp.float32), precision=lax.Precision.HIGHEST) * scale
    delta_parent = jnp.einsum('ocd,nocq->ndq', up_weight.astype(jnp.float32), du8, precision=lax.Precision.HIGHEST).astype(jnp.bfloat16)

    def slot_grads(pair):
        grid_block, cell_block = pair
        return jnp.take(grid_block, cell_block, axis=1)
    per_receiver = lax.map(slot_grads, (delta_parent, recv_cell))
    per_sender = per_receiver.reshape(devices_all, C, devices_all, CAP).transpose(2, 1, 0, 3).reshape(devices_all, C, SLOTS)
    grad_parent = jnp.where(live[:, None, :], per_sender, jnp.zeros_like(per_sender))
    return (decoded, grad_parent, grad_one, grad_two, grad_up)
```

```python
import functools
import math

import jax
import jax.numpy as jnp
from jax import lax
from jax.experimental import pallas as pl
from jax.experimental.pallas import tpu as pltpu
from jax.sharding import PartitionSpec as P

BF = jnp.bfloat16
F32 = jnp.float32
XK = (0, 1, 2, -1, -2, 3)
C = 64
Z = 128
Y = 8
K = 64
DEV = 128
NO_CELL = 256.0
STEP = 8


def iota(shape, dim):
    return lax.broadcasted_iota(jnp.int32, shape, dim)


def ones_where(cond):
    return jnp.where(cond, 1.0, 0.0).astype(BF)


def nt(a, b):
    return lax.dot_general(a, b, (((1,), (1,)), ((), ())), preferred_element_type=F32)


def nn(a, b):
    return lax.dot_general(a, b, (((1,), (0,)), ((), ())), preferred_element_type=F32)


def tn(a, b):
    return lax.dot_general(a, b, (((0,), (0,)), ((), ())), preferred_element_type=F32)


def over(total, body, step=STEP):
    full = total // step

    def one(i, carry):
        body(pl.multiple_of(i * step, step), step)
        return carry

    lax.fori_loop(0, full, one, 0)
    if total % step:
        body(full * step, total % step)


def low_lanes(shape):
    return iota(shape, len(shape) - 1) < C


def stack_y(block):
    count, rows, lanes = block.shape
    row = iota(block.shape, 1)
    below = jnp.where(row == 0, 0.0, pltpu.roll(block, 1, 1))
    above = jnp.where(row == rows - 1, 0.0, pltpu.roll(block, rows - 1, 1))
    wide = jnp.concatenate([below, block, above], axis=2)
    return wide.reshape(count * rows, 3 * lanes).astype(BF)


def call(kernel, outs, scratch=(), limit=58 << 20):
    single = isinstance(outs, tuple)
    shapes = [jax.ShapeDtypeStruct(s, d) for s, d in ([outs] if single else outs)]
    vmem = pl.BlockSpec(memory_space=pltpu.VMEM)

    def run(*args):
        got = pl.pallas_call(
            kernel,
            out_shape=shapes,
            in_specs=[vmem] * len(args),
            out_specs=[vmem] * len(shapes),
            scratch_shapes=[pltpu.VMEM(s, d) for s, d in scratch],
            compiler_params=pltpu.CompilerParams(vmem_limit_bytes=limit),
        )(*args)
        return got[0] if single else got

    return run


def weights_kernel(up_ref, one_ref, two_ref, w1_ref, w2_ref, b1_ref, b0_ref, u_ref, ud_ref):
    zero = jnp.zeros((C, C), BF)

    def tap(ref, ox, oy, oz):
        return zero if abs(ox) > 1 else ref[9 * (ox + 1) + 3 * (oy + 1) + oz + 1]

    def join(a, b):
        return jnp.concatenate([a, b], axis=1)

    for oz in (-1, 0, 1):
        for oy in (-1, 0, 1):
            for n, xo in enumerate((0, 1, 2, -1)):
                rows = slice(n * C, n * C + C)
                for p in range(3):
                    at = (oy + 1) * 384 + p * 128
                    pair = [tap(one_ref, XK[2 * p + s] - xo, oy, oz) for s in (0, 1)]
                    w1_ref[oz + 1, rows, at : at + 128] = join(*pair)
            for n, xo in enumerate((0, 1)):
                at_row = (oz + 1) * 128 + n * C
                for p in range(2):
                    at = (oy + 1) * 256 + p * 128
                    pair = [tap(two_ref, XK[2 * p + s] - xo, oy, oz) for s in (0, 1)]
                    w2_ref[at_row : at_row + C, at : at + 128] = join(*pair)
            for kk, xk in enumerate(XK):
                at_row = (oy + 1) * 384 + kk * C
                for p, pair in enumerate(((0, 1), (2, -1))):
                    b1_ref[oz + 1, at_row : at_row + C, p * 128 : p * 128 + 128] = join(
                        *[tap(two_ref, xo - xk, -oy, -oz) for xo in pair]
                    )
            for kk, xk in enumerate(XK[:4]):
                at_row = (oy + 1) * 256 + kk * C
                at = (oz + 1) * 128
                b0_ref[at_row : at_row + C, at : at + 128] = join(
                    *[tap(one_ref, xo - xk, -oy, -oz) for xo in (0, 1)]
                )
    for e in (0, 1):
        for b in (0, 1):
            for a in (0, 1):
                at = (e * 4 + b * 2 + a) * C
                u_ref[at : at + C, :] = join(up_ref[4 * a + 2 * b + e], zero)
        for a in (0, 1):
            at = 512 + (e * 2 + a) * C
            u_ref[at : at + C, :] = ones_where(iota((C, 128), 1) == C + 2 * a + e)
            ud_ref[e, a * C : a * C + C, :] = join(up_ref[4 * a + e], up_ref[4 * a + 2 + e])


def send_kernel(feat_ref, cell_ref, count_ref, out_ref):
    spread = ones_where((iota((DEV, 2048), 1) >> 4) == iota((DEV, 2048), 0))
    count = jnp.broadcast_to(count_ref[...].astype(F32), (8, DEV)).astype(BF)
    counts = nn(count, spread)[0:1]
    slot = (iota((1, 2048), 1) & 15).astype(F32)
    cell = jnp.where(slot < counts, cell_ref[...].astype(F32), NO_CELL)
    for chunk in range(16):
        at = slice(chunk * 128, chunk * 128 + 128)
        feats = feat_ref[0, :, at].astype(F32)
        cells = jnp.broadcast_to(cell[:, at], (C, 128))
        turned = jnp.concatenate([feats, cells], axis=0).T.reshape(8, 2, 8, 128)
        first, second = turned[:, 0], turned[:, 1]
        low = low_lanes(first.shape)
        to = slice(chunk * 8, chunk * 8 + 8)
        out_ref[to, 0:8, :] = jnp.where(low, first, pltpu.roll(second, C, 2)).astype(BF)
        out_ref[to, 8:16, :] = jnp.where(low, pltpu.roll(first, C, 2), second).astype(BF)


def onehots(recv_ref):
    cells = recv_ref[:, 8:16, :].astype(F32).reshape(1024, 128)
    ids = iota((1024, 256), 1).astype(F32)
    return ones_where(cells[:, 0:1] == ids), ones_where(cells[:, C : C + 1] == ids)


def grid_kernel(recv_ref, mask_ref, cot_ref, rec_ref, up_ref, down_ref):
    feats = recv_ref[:, 0:8, :].astype(F32).reshape(1024, 128).astype(BF)
    both = tn(feats, jnp.concatenate(onehots(recv_ref), axis=1))
    grid = both[0:C, 0:256] + both[C:128, 256:512]
    grid = jnp.concatenate([grid, jnp.zeros((C, 256), F32)], axis=0).astype(BF)
    row, col = iota((512, 256), 0), iota((512, 256), 1)
    pick = ones_where(col == ((row & 7) >> 1) * K + (row >> 3))
    rec = nt(pick, grid)
    kk, zz = iota((K, Y, Z), 0), iota((K, Y, Z), 2)
    zrow, lane = iota((Z, 128), 0), iota((Z, 128), 1)
    for a in (0, 1):
        mine = jnp.where((zz >> 1) == kk, mask_ref[a].astype(F32)[None], 0.0)
        place = ones_where(lane == C + 2 * a + (zrow & 1))
        rec = rec + nn(mine.reshape(512, Z).astype(BF), place)
    rec = rec.reshape(K, Y, 128).astype(BF)
    rec_ref[...] = rec
    up_ref[0:2] = rec_ref[K - 2 : K]
    up_ref[2:4] = cot_ref[Z - 2 : Z]
    down_ref[0:2] = rec_ref[0:2]
    down_ref[2:4] = cot_ref[0:2]


def lane_groups(own, left, right):
    low = low_lanes(own.shape)
    return own, jnp.where(low, right, left), jnp.where(low, left, right)


def forward_kernel(
    own_ref, left_ref, right_ref, cot_ref, u_ref, w1_ref, w2_ref,
    act_ref, delta_ref, dec_ref, slope_ref, lifted_ref, keep_ref,
    lift, seen, mask, col1, part1, col2, part2,
):
    kz = own_ref.shape[0]
    odd_row = (iota((kz, Y, 128), 1) & 1) == 1
    for t, ref in enumerate((own_ref, left_ref, right_ref)):
        rec = ref[...].astype(F32).reshape(kz * Y, 128).astype(BF)
        for e in (0, 1):
            both = nt(rec, u_ref[e * 256 : e * 256 + 256, :]).reshape(kz, Y, 256)
            live = nt(rec, u_ref[512 + e * 128 : 640 + e * 128, :]).reshape(kz, Y, 128)
            lift[t, :, e] = live * jnp.where(odd_row, both[:, :, 128:], both[:, :, :128])
            seen[t, :, e] = live

    def columns(k0, n):
        def load(ref):
            return lane_groups(*[ref[t, pl.ds(k0, n)].reshape(2 * n, Y, 128) for t in range(3)])

        own, near, far = load(lift)
        at = pl.ds(2 * k0, 2 * n)
        lifted_ref[at] = jnp.concatenate([own, near], axis=2).astype(BF)
        rows = pl.ds(pl.multiple_of(k0 * 16, 16), 16 * n)
        col1[rows, :] = stack_y(jnp.concatenate([own, near, far], axis=2))
        live_own, live_near, _ = load(seen)
        mask[at] = jnp.concatenate([live_own, live_near], axis=2)

    over(kz, columns, 4)
    for s in range(3):
        part1[s] = nt(col1[...], w1_ref[s]).reshape(2 * kz, Y, 256)

    def first(m, n):
        pre = part1[0, pl.ds(m, n)] + part1[1, pl.ds(m + 1, n)] + part1[2, pl.ds(m + 2, n)]
        live = mask[pl.ds(m + 1, n)]
        sig = jax.nn.sigmoid(pre)
        act = live * (pre * sig)
        slope_ref[pl.ds(m, n)] = live * (sig * (1.0 + pre * (1.0 - sig)))
        act_ref[pl.ds(m, n)] = act.astype(BF)
        col2[pl.ds(pl.multiple_of(m * Y, 16), n * Y), :] = stack_y(act)

    over(2 * kz - 2, first)
    part2[...] = nt(col2[...], w2_ref[...]).reshape(2 * kz - 2, Y, 384)

    def second(q, n):
        pre = (
            part2[pl.ds(q, n), :, 0:128]
            + part2[pl.ds(q + 1, n), :, 128:256]
            + part2[pl.ds(q + 2, n), :, 256:384]
        )
        live = mask[pl.ds(q + 2, n), :, 0:128]
        sig = jax.nn.sigmoid(pre)
        at = pl.ds(q, n)
        dec_ref[at] = (live * (pre * sig)).astype(BF)
        slope = live * (sig * (1.0 + pre * (1.0 - sig)))
        delta_ref[at] = (cot_ref[at].astype(F32) * slope).astype(BF)
        keep_ref[at] = live.astype(BF)

    over(2 * kz - 4, second)


def wgrad(count, field, padded, shifted, col):
    def build(m, n):
        three = [padded[pl.ds(m + s, n)] for s in (2, 1, 0)]
        rows = pl.ds(pl.multiple_of(m * Y, 16), n * Y)
        shifted[rows, :] = jnp.concatenate(three, axis=2).reshape(n * Y, 384).astype(BF)
        col[rows, :] = stack_y(field(m, n))

    over(count, build)
    return tn(shifted[...], col[...])


def packed(block):
    return jnp.concatenate([block[0:32], block[32:64]], axis=1).astype(BF)


def tap_grads(total, put):
    place = {0: 0, 1: 1, 2: 2, -1: 3}
    for ox in (-1, 0, 1):
        for oy in (-1, 0, 1):
            for oz in (-1, 0, 1):
                sums = []
                for x in (0, 1):
                    r = (oz + 1) * 128 + x * C
                    c = (oy + 1) * 256 + place[x + ox] * C
                    sums.append(total[r : r + C, c : c + C])
                put(9 * (ox + 1) + 3 * (oy + 1) + oz + 1, packed(sums[0] + sums[1]))


def second_grad_kernel(act_ref, delta_ref, out_ref, padded, shifted, col, total):
    padded[0:4] = jnp.zeros((4, Y, 128), F32)
    padded[132:136] = jnp.zeros((4, Y, 128), F32)
    padded[4:132] = delta_ref[2:130].astype(F32)
    total[...] = wgrad(134, lambda m, n: act_ref[pl.ds(m, n)].astype(F32), padded, shifted, col)

    def put(t, block):
        out_ref[t] = block

    tap_grads(total, put)


def backward_kernel(
    own_ref, left_ref, right_ref, slope_ref, keep_ref, lifted_ref, rec_ref, recv_ref,
    b1_ref, b0_ref, ud_ref, two_ref, out_ref,
    col3, part3, col4, part4, padded, shifted, col, total, du,
):
    def columns(q, n):
        at = pl.ds(q, n)
        groups = lane_groups(*[r[at].astype(F32) for r in (own_ref, left_ref, right_ref)])
        rows = pl.ds(pl.multiple_of(q * Y, 16), n * Y)
        col3[rows, :] = stack_y(jnp.concatenate(groups, axis=2))

    over(132, columns)
    for s in range(3):
        part3[s] = nn(col3[...], b1_ref[s]).reshape(132, Y, 256)

    def first(r, n):
        back = part3[0, pl.ds(r, n)] + part3[1, pl.ds(r + 1, n)] + part3[2, pl.ds(r + 2, n)]
        delta = back * slope_ref[pl.ds(r + 2, n)]
        padded[pl.ds(r + 2, n)] = delta[:, :, 0:128]
        col4[pl.ds(pl.multiple_of(r * Y, 16), n * Y), :] = stack_y(delta)

    over(130, first)
    padded[0:3] = jnp.zeros((3, Y, 128), F32)
    padded[131:134] = jnp.zeros((3, Y, 128), F32)
    part4[...] = nn(col4[...], b0_ref[...]).reshape(130, Y, 384)

    def upper(z, n):
        back = (
            part4[pl.ds(z, n), :, 0:128]
            + part4[pl.ds(z + 1, n), :, 128:256]
            + part4[pl.ds(z + 2, n), :, 256:384]
        )
        value = keep_ref[pl.ds(z + 2, n)].astype(F32) * back
        du[pl.ds(z >> 1, n // 2)] = value.reshape(n // 2, 2, Y, 128)

    over(Z, upper)

    split = [du[:, e].reshape(K * Y, 128).astype(BF) for e in (0, 1)]
    row, lane = iota((K * Y, 128), 0), iota((K * Y, 128), 1)
    match = ((row & 1) == 0) == (lane < C)
    summed = nn(split[0], ud_ref[0]) + nn(split[1], ud_ref[1])
    summed = jnp.where(match, summed, 0.0).reshape(K, Y, 128)
    summed = summed + pltpu.roll(summed, Y - 1, 1)
    summed = summed + pltpu.roll(summed, C, 2)
    parent = summed.reshape(K * Y, 128).astype(BF)
    cell, src = iota((256, 512), 0), iota((256, 512), 1)
    pick = ones_where(src == (cell & (K - 1)) * Y + 2 * (cell >> 6))
    parent = nn(pick, parent).astype(BF)
    slots = [nn(hot, parent) for hot in onehots(recv_ref)]
    slots = jnp.where(iota((1024, 128), 1) < C, slots[0], slots[1])
    out_ref[:, 0:8, :] = slots.reshape(DEV, 8, 128).astype(BF)

    def put(index, block):
        out_ref[2 * index, 8:24, :] = block[0:16]
        out_ref[2 * index + 1, 8:24, :] = block[16:32]

    rec = rec_ref[...].astype(F32).reshape(K * Y, 128)
    rec = jnp.where(lane < C, rec, pltpu.roll(rec, C, 1))
    rec = jnp.where(match, rec, 0.0).astype(BF)
    for e in (0, 1):
        up_grad = tn(split[e], rec)
        for a in (0, 1):
            for b in (0, 1):
                block = up_grad[a * C : a * C + C, b * C : b * C + C]
                put(54 + 4 * a + 2 * b + e, packed(block))
    total[...] = wgrad(
        132, lambda m, n: lifted_ref[pl.ds(m + 2, n)].astype(F32), padded, shifted, col
    )
    tap_grads(total, lambda t, block: put(27 + t, block))
    for t in range(27):
        put(t, two_ref[t])
    out_ref[124:128, 8:24, :] = jnp.zeros((4, 16, 128), BF)


def sum_kernel(recv_ref, out_ref, *, scale):
    def one(i, total):
        return total + jnp.sum(recv_ref[pl.ds(i * 8, 8), 8:24, :].astype(F32), axis=0)

    total = lax.fori_loop(0, 16, one, jnp.zeros((16, 128), F32))
    out_ref[...] = jnp.broadcast_to((total * scale).astype(BF)[None], out_ref.shape)


def slot_kernel(recv_ref, out_ref):
    for chunk in range(16):
        block = recv_ref[chunk * 8 : chunk * 8 + 8, 0:8, :].astype(F32)
        halves = [block[:, None], pltpu.roll(block, C, 2)[:, None]]
        turned = jnp.concatenate(halves, axis=1).reshape(128, 128).T
        out_ref[0, :, chunk * 128 : chunk * 128 + 128] = turned[0:C].astype(BF)


def unpack_kernel(recv_ref, one_ref, two_ref, up_ref):
    def matrix(index):
        top = recv_ref[2 * index].astype(F32)
        low = recv_ref[2 * index + 1].astype(F32)
        both = jnp.concatenate([top, low], axis=0)
        return jnp.concatenate([both[:, :C], both[:, C:]], axis=0)

    for t in range(27):
        two_ref[t] = matrix(t)
        one_ref[t] = matrix(27 + t)
    for o in range(8):
        up_ref[o] = matrix(54 + o)


def shift(array, axis, step):
    count = lax.axis_size(axis)
    pairs = [(i, i + step) for i in range(count) if 0 <= i + step < count]
    return lax.ppermute(array, axis, pairs)


def exchange(array):
    return lax.all_to_all(array, ("gz", "xy"), 0, 0, tiled=True)


def local(
    parent_feat, parent_cell, send_count, up_weight, conv_one, conv_two, child_mask, cotangent
):
    size_x, size_y, size_z = cotangent.shape[1:]
    voxels = size_x * size_y * size_z * lax.axis_size("xy") * lax.axis_size("gz")
    scale = 1.0 / math.sqrt(voxels)
    kz = K + 4

    sent = call(send_kernel, ((DEV, 16, 128), BF))(parent_feat, parent_cell, send_count)
    recv = exchange(sent)
    cot = cotangent.transpose(3, 2, 1, 0).reshape(Z, Y, 128)
    w1, w2, b1, b0, u, ud = call(
        weights_kernel,
        [
            ((3, 256, 1152), BF), ((384, 768), BF), ((3, 1152, 256), BF), ((768, 384), BF),
            ((768, 128), BF), ((2, 128, 128), BF),
        ],
    )(up_weight, conv_one, conv_two)
    rec, up_edge, down_edge = call(
        grid_kernel, [((K, Y, 128), BF), ((4, Y, 128), BF), ((4, Y, 128), BF)]
    )(recv, child_mask, cot)
    before = shift(up_edge, "gz", 1)
    after = shift(down_edge, "gz", -1)
    rec_ext = jnp.concatenate([before[0:2], rec, after[0:2]], axis=0)
    cot_ext = jnp.concatenate([before[2:4], cot, after[2:4]], axis=0)
    rec_left, rec_right = shift(rec_ext, "xy", 1), shift(rec_ext, "xy", -1)
    act, delta, dec, slope, lifted, keep = call(
        forward_kernel,
        [
            ((134, Y, 256), BF), ((132, Y, 128), BF), ((132, Y, 128), BF),
            ((134, Y, 256), F32), ((136, Y, 256), BF), ((132, Y, 128), BF),
        ],
        [
            ((3, kz, 2, Y, 128), F32), ((3, kz, 2, Y, 128), F32), ((136, Y, 256), F32),
            ((1088, 1152), BF), ((3, 136, Y, 256), F32), ((1072, 768), BF), ((134, Y, 384), F32),
        ],
    )(rec_ext, rec_left, rec_right, cot_ext, u, w1, w2)
    delta_left, delta_right = shift(delta, "xy", 1), shift(delta, "xy", -1)
    two = call(
        second_grad_kernel,
        ((27, 32, 128), BF),
        [((136, Y, 128), F32), ((1072, 384), BF), ((1072, 768), BF), ((384, 768), F32)],
    )(act, delta)
    decoded = dec[2 : 2 + Z].reshape(Z, Y, 2, C).transpose(3, 2, 1, 0)
    message = call(
        backward_kernel,
        ((DEV, 24, 128), BF),
        [
            ((1056, 1152), BF), ((3, 132, Y, 256), F32), ((1040, 768), BF), ((130, Y, 384), F32),
            ((134, Y, 128), F32), ((1056, 384), BF), ((1056, 768), BF), ((384, 768), F32),
            ((K, 2, Y, 128), F32),
        ],
    )(
        delta, delta_left, delta_right, slope, keep, lifted, rec, recv, b1, b0, ud, two
    )
    back = exchange(message)
    total = call(functools.partial(sum_kernel, scale=scale), ((DEV, 16, 128), BF))(back)
    gathered = exchange(total)
    grad_parent = call(slot_kernel, ((1, C, 2048), BF))(back)
    grad_one, grad_two, grad_up = call(
        unpack_kernel, [((27, C, C), F32), ((27, C, C), F32), ((8, C, C), F32)]
    )(gathered)
    return decoded, grad_parent, grad_one, grad_two, grad_up


def solution(mesh):
    placed = (
        P(("gz", "xy"), None, None),
        P(("gz", "xy"), None),
        P(("gz", "xy"), None),
        P(),
        P(),
        P(),
        P("xy", None, "gz"),
        P(None, "xy", None, "gz"),
    )
    return jax.shard_map(
        local,
        mesh=mesh,
        in_specs=placed,
        out_specs=(P(None, "xy", None, "gz"), P(("gz", "xy"), None, None), P(), P(), P()),
        check_vma=False,
    )
```

```python
import functools
import math

import jax
import jax.numpy as jnp
from jax import lax
from jax.experimental import pallas as pl
from jax.experimental.pallas import tpu as pltpu
from jax.sharding import PartitionSpec as P

BF = jnp.bfloat16
F32 = jnp.float32
XK = (0, 1, 2, -1, -2, 3)
C = 64
Z = 128
Y = 8
K = 64
KZ = K + 4
DEV = 128
NO_CELL = 256.0
STEP = 8


def iota(shape, dim):
    return lax.broadcasted_iota(jnp.int32, shape, dim)


def ones_where(cond):
    return jnp.where(cond, 1.0, 0.0).astype(BF)


def nt(a, b):
    return lax.dot_general(a, b, (((1,), (1,)), ((), ())), preferred_element_type=F32)


def nn(a, b):
    return lax.dot_general(a, b, (((1,), (0,)), ((), ())), preferred_element_type=F32)


def tn(a, b):
    return lax.dot_general(a, b, (((0,), (0,)), ((), ())), preferred_element_type=F32)


def over(total, body, step=STEP):
    full = total // step

    def one(i, carry):
        body(pl.multiple_of(i * step, step), step)
        return carry

    lax.fori_loop(0, full, one, 0)
    if total % step:
        body(full * step, total % step)


def low_lanes(shape):
    return iota(shape, len(shape) - 1) < C


def stack_y(block):
    count, rows, lanes = block.shape
    row = iota(block.shape, 1)
    below = jnp.where(row == 0, 0.0, pltpu.roll(block, 1, 1))
    above = jnp.where(row == rows - 1, 0.0, pltpu.roll(block, rows - 1, 1))
    wide = jnp.concatenate([below, block, above], axis=2)
    return wide.reshape(count * rows, 3 * lanes).astype(BF)


def call(kernel, outs, scratch=(), home=False, raw=False, limit=22 << 20):
    single = isinstance(outs, tuple)
    listed = [outs] if single else outs
    home = home if isinstance(home, tuple) else (home,) * len(listed)
    shapes = [
        jax.ShapeDtypeStruct(s, d) if h else pltpu.VMEM(s, d) for (s, d), h in zip(listed, home)
    ]
    vmem = pl.BlockSpec(memory_space=pltpu.VMEM)

    def run(*args):
        if not raw:
            args = [pltpu.with_memory_space_constraint(a, pltpu.VMEM) for a in args]
        got = pl.pallas_call(
            kernel,
            out_shape=shapes,
            in_specs=[vmem] * len(args),
            out_specs=[vmem] * len(shapes),
            scratch_shapes=[pltpu.VMEM(s, d) for s, d in scratch],
            compiler_params=pltpu.CompilerParams(vmem_limit_bytes=limit),
        )(*args)
        return got[0] if single else got

    return run


def dot_rows(dot, rows_ref, weights, put):
    total = rows_ref.shape[0]
    half = (total // 2 + 15) // 16 * 16
    for start, stop in ((0, half), (half, total)):
        got = dot(rows_ref[start:stop], weights)
        put(slice(start // Y, stop // Y), got.reshape((stop - start) // Y, Y, got.shape[1]))


def tap(ref, ox, oy, oz):
    if abs(ox) > 1:
        return jnp.zeros((C, C), BF)
    return ref[9 * (ox + 1) + 3 * (oy + 1) + oz + 1]


def join(a, b):
    return jnp.concatenate([a, b], axis=1)


def forward_weights(up_ref, one_ref, two_ref, w1o_ref, w1x_ref, w2_ref, u_ref):
    zero = jnp.zeros((C, C), BF)
    for oz in (-1, 0, 1):
        for oy in (-1, 0, 1):
            for n, xo in enumerate((0, 1, 2, -1)):
                rows = slice(n * C, n * C + C)
                for p in range(3):
                    ref, at = w1o_ref, (oy + 1) * 128
                    if p:
                        ref, at = w1x_ref, (oy + 1) * 256 + p * 128 - 128
                    pair = [tap(one_ref, XK[2 * p + s] - xo, oy, oz) for s in (0, 1)]
                    ref[oz + 1, rows, at : at + 128] = join(*pair)
            for n, xo in enumerate((0, 1)):
                at_row = (oz + 1) * 128 + n * C
                for p in range(2):
                    at = (oy + 1) * 256 + p * 128
                    pair = [tap(two_ref, XK[2 * p + s] - xo, oy, oz) for s in (0, 1)]
                    w2_ref[at_row : at_row + C, at : at + 128] = join(*pair)
    for e in (0, 1):
        for a in (0, 1):
            for b in (0, 1):
                at = (e * 4 + b * 2 + a) * C
                u_ref[at : at + C, :] = join(up_ref[4 * a + 2 * b + e], zero)
            at = 512 + (e * 2 + a) * C
            u_ref[at : at + C, :] = ones_where(iota((C, 128), 1) == C + 2 * a + e)


def backward_weights(up_ref, one_ref, two_ref, b1o_ref, b1x_ref, b0_ref, ud_ref):
    for oz in (-1, 0, 1):
        for oy in (-1, 0, 1):
            for kk, xk in enumerate(XK):
                ref, at_row = b1x_ref, (oy + 1) * 256 + kk * C - 128
                if kk < 2:
                    ref, at_row = b1o_ref, (oy + 1) * 128 + kk * C
                for p, pair in enumerate(((0, 1), (2, -1))):
                    ref[oz + 1, at_row : at_row + C, p * 128 : p * 128 + 128] = join(
                        *[tap(two_ref, xo - xk, -oy, -oz) for xo in pair]
                    )
            for kk, xk in enumerate(XK[:4]):
                at_row = (oy + 1) * 256 + kk * C
                at = (oz + 1) * 128
                b0_ref[at_row : at_row + C, at : at + 128] = join(
                    *[tap(one_ref, xo - xk, -oy, -oz) for xo in (0, 1)]
                )
    for e in (0, 1):
        for a in (0, 1):
            ud_ref[e, a * C : a * C + C, :] = join(up_ref[4 * a + e], up_ref[4 * a + 2 + e])


def send_kernel(feat_ref, cell_ref, count_ref, out_ref):
    spread = ones_where((iota((DEV, 2048), 1) >> 4) == iota((DEV, 2048), 0))
    count = jnp.broadcast_to(count_ref[...].astype(F32), (8, DEV)).astype(BF)
    counts = nn(count, spread)[0:1]
    slot = (iota((1, 2048), 1) & 15).astype(F32)
    cell = jnp.where(slot < counts, cell_ref[...].astype(F32), NO_CELL)
    for chunk in range(16):
        at = slice(chunk * 128, chunk * 128 + 128)
        feats = feat_ref[0, :, at].astype(F32)
        cells = jnp.broadcast_to(cell[:, at], (C, 128))
        turned = jnp.concatenate([feats, cells], axis=0).T.reshape(8, 2, 8, 128)
        first, second = turned[:, 0], turned[:, 1]
        low = low_lanes(first.shape)
        to = slice(chunk * 8, chunk * 8 + 8)
        out_ref[to, 0:8, :] = jnp.where(low, first, pltpu.roll(second, C, 2)).astype(BF)
        out_ref[to, 8:16, :] = jnp.where(low, pltpu.roll(first, C, 2), second).astype(BF)


def onehots(recv_ref):
    cells = recv_ref[:, 8:16, :].astype(F32).reshape(1024, 128)
    ids = iota((1024, 256), 1).astype(F32)
    return ones_where(cells[:, 0:1] == ids), ones_where(cells[:, C : C + 1] == ids)


def grid_kernel(recv_ref, mask_ref, cot_ref, rec_ref, up_ref, down_ref):
    feats = recv_ref[:, 0:8, :].astype(F32).reshape(1024, 128).astype(BF)
    both = tn(feats, jnp.concatenate(onehots(recv_ref), axis=1))
    grid = both[0:C, 0:256] + both[C:128, 256:512]
    grid = jnp.concatenate([grid, jnp.zeros((C, 256), F32)], axis=0).astype(BF)
    row, col = iota((512, 256), 0), iota((512, 256), 1)
    pick = ones_where(col == ((row & 7) >> 1) * K + (row >> 3))
    rec = nt(pick, grid)
    kk, zz = iota((K, Y, Z), 0), iota((K, Y, Z), 2)
    zrow, lane = iota((Z, 128), 0), iota((Z, 128), 1)
    for a in (0, 1):
        mine = jnp.where((zz >> 1) == kk, mask_ref[a].astype(F32)[None], 0.0)
        place = ones_where(lane == C + 2 * a + (zrow & 1))
        rec = rec + nn(mine.reshape(512, Z).astype(BF), place)
    rec = rec.reshape(K, Y, 128).astype(BF)
    rec_ref[...] = rec
    up_ref[0:2] = rec_ref[K - 2 : K]
    up_ref[2:4] = cot_ref[Z - 2 : Z]
    down_ref[0:2] = rec_ref[0:2]
    down_ref[2:4] = cot_ref[0:2]


def lane_groups(own, left, right):
    low = low_lanes(own.shape)
    return own, jnp.where(low, right, left), jnp.where(low, left, right)


def lift_tile(rec_ref, u_ref, lift, seen):
    kz = rec_ref.shape[0]
    rec = rec_ref[...].astype(F32).reshape(kz * Y, 128).astype(BF)
    odd_row = (iota((kz, Y, 128), 1) & 1) == 1
    for e in (0, 1):
        both = nt(rec, u_ref[e * 256 : e * 256 + 256, :]).reshape(kz, Y, 256)
        live = nt(rec, u_ref[512 + e * 128 : 640 + e * 128, :]).reshape(kz, Y, 128)
        lift[:, e] = live * jnp.where(odd_row, both[:, :, 128:], both[:, :, :128])
        seen[:, e] = live


def own_kernel(
    rec_ref, up_ref, one_ref, two_ref, lift, seen, part, u_ref, w1x_ref, w2_ref, w1o_ref, col
):
    forward_weights(up_ref, one_ref, two_ref, w1o_ref, w1x_ref, w2_ref, u_ref)
    lift_tile(rec_ref, u_ref, lift, seen)

    def columns(k0, n):
        own = lift[pl.ds(k0, n)].reshape(2 * n, Y, 128)
        col[pl.ds(pl.multiple_of(k0 * 16, 16), 16 * n), :] = stack_y(own)

    over(KZ, columns, 4)
    for s in range(3):

        def keep(at, value, s=s):
            part[s, at] = value

        dot_rows(nt, col, w1o_ref[s], keep)


def forward_kernel(
    left_ref, right_ref, before_ref, after_ref, cot_in_ref,
    lift_own, seen_own, part_own, u_ref, w1x_ref, w2_ref,
    act_ref, delta_ref, dec_ref, slope_ref, lifted_ref, keep_ref,
    lift, seen, mask, col1, part1, col2, part2, cot_ref,
):
    kz = KZ
    cot_ref[0:2] = before_ref[2:4]
    cot_ref[2 : 2 + Z] = cot_in_ref[...]
    cot_ref[2 + Z : 4 + Z] = after_ref[2:4]
    for t, ref in enumerate((left_ref, right_ref)):
        lift_tile(ref, u_ref, lift.at[t], seen.at[t])

    def columns(k0, n):
        def load(own_ref, ref):
            three = [own_ref[pl.ds(k0, n)], ref[0, pl.ds(k0, n)], ref[1, pl.ds(k0, n)]]
            return lane_groups(*[v.reshape(2 * n, Y, 128) for v in three])

        own, near, far = load(lift_own, lift)
        at = pl.ds(2 * k0, 2 * n)
        lifted_ref[at] = jnp.concatenate([own, near], axis=2).astype(BF)
        rows = pl.ds(pl.multiple_of(k0 * 16, 16), 16 * n)
        col1[rows, :] = stack_y(jnp.concatenate([near, far], axis=2))
        live_own, live_near, _ = load(seen_own, seen)
        mask[at] = jnp.concatenate([live_own, live_near], axis=2)

    over(kz, columns, 4)
    for s in range(3):

        def keep1(at, value, s=s):
            part1[s, at] = part_own[s, at] + value

        dot_rows(nt, col1, w1x_ref[s], keep1)

    def first(m, n):
        pre = part1[0, pl.ds(m, n)] + part1[1, pl.ds(m + 1, n)] + part1[2, pl.ds(m + 2, n)]
        live = mask[pl.ds(m + 1, n)]
        sig = jax.nn.sigmoid(pre)
        act = live * (pre * sig)
        slope_ref[pl.ds(m, n)] = live * (sig * (1.0 + pre * (1.0 - sig)))
        act_ref[pl.ds(m, n)] = act.astype(BF)
        col2[pl.ds(pl.multiple_of(m * Y, 16), n * Y), :] = stack_y(act)

    over(2 * kz - 2, first)

    def keep2(at, value):
        part2[at] = value

    dot_rows(nt, col2, w2_ref[...], keep2)

    def second(q, n):
        pre = (
            part2[pl.ds(q, n), :, 0:128]
            + part2[pl.ds(q + 1, n), :, 128:256]
            + part2[pl.ds(q + 2, n), :, 256:384]
        )
        live = mask[pl.ds(q + 2, n), :, 0:128]
        sig = jax.nn.sigmoid(pre)
        at = pl.ds(q, n)
        dec_ref[at] = (live * (pre * sig)).astype(BF)
        slope = live * (sig * (1.0 + pre * (1.0 - sig)))
        delta_ref[at] = (cot_ref[at].astype(F32) * slope).astype(BF)
        keep_ref[at] = live.astype(BF)

    over(2 * kz - 4, second)


def wgrad(count, also, padded, shifted, col):
    def build(m, n):
        three = [padded[pl.ds(m + s, n)] for s in (2, 1, 0)]
        rows = pl.ds(pl.multiple_of(m * Y, 16), n * Y)
        shifted[rows, :] = jnp.concatenate(three, axis=2).reshape(n * Y, 384).astype(BF)
        also(rows, m, n)

    over(count, build)
    return tn(shifted[...], col[...])


def packed(block):
    return jnp.concatenate([block[0:32], block[32:64]], axis=1).astype(BF)


def tap_grads(total, put):
    place = {0: 0, 1: 1, 2: 2, -1: 3}
    for ox in (-1, 0, 1):
        for oy in (-1, 0, 1):
            for oz in (-1, 0, 1):
                sums = []
                for x in (0, 1):
                    r = (oz + 1) * 128 + x * C
                    c = (oy + 1) * 256 + place[x + ox] * C
                    sums.append(total[r : r + C, c : c + C])
                put(9 * (ox + 1) + 3 * (oy + 1) + oz + 1, packed(sums[0] + sums[1]))


def second_grad_kernel(
    act_ref, delta_ref, recv_ref, lifted_ref, dec_ref, up_ref, one_ref, two_ref,
    out_ref, hot_ref, part_ref, lifted_col, dec_out, b1x_ref, b0_ref, ud_ref,
    b1o_ref, padded, shifted, col, total, col3,
):
    hot_ref[...] = jnp.concatenate(onehots(recv_ref), axis=1)
    dec_out[...] = dec_ref[2 : 2 + Z]
    backward_weights(up_ref, one_ref, two_ref, b1o_ref, b1x_ref, b0_ref, ud_ref)

    def columns(q, n):
        rows = pl.ds(pl.multiple_of(q * Y, 16), n * Y)
        col3[rows, :] = stack_y(delta_ref[pl.ds(q, n)].astype(F32))
        lifted_col[rows, :] = stack_y(lifted_ref[pl.ds(q + 2, n)].astype(F32))

    over(132, columns)
    for s in range(3):

        def keep(at, value, s=s):
            part_ref[s, at] = value

        dot_rows(nn, col3, b1o_ref[s], keep)
    padded[0:4] = jnp.zeros((4, Y, 128), F32)
    padded[132:136] = jnp.zeros((4, Y, 128), F32)
    padded[4:132] = delta_ref[2:130].astype(F32)
    def act_col(rows, m, n):
        col[rows, :] = stack_y(act_ref[pl.ds(m, n)].astype(F32))

    total[...] = wgrad(134, act_col, padded, shifted, col)

    def put(t, block):
        out_ref[t] = block

    tap_grads(total, put)


def backward_kernel(
    left_ref, right_ref, slope_ref, keep_ref, rec_ref, hot_ref, part_own, lifted_col, two_ref,
    b1x_ref, b0_ref, ud_ref, out_ref,
    col3, part3, col4, part4, padded, shifted, total, du,
):
    def columns(q, n):
        at = pl.ds(q, n)
        left, right = left_ref[at].astype(F32), right_ref[at].astype(F32)
        groups = lane_groups(left, left, right)[1:]
        rows = pl.ds(pl.multiple_of(q * Y, 16), n * Y)
        col3[rows, :] = stack_y(jnp.concatenate(groups, axis=2))

    over(132, columns)
    for s in range(3):

        def keep3(at, value, s=s):
            part3[s, at] = part_own[s, at] + value

        dot_rows(nn, col3, b1x_ref[s], keep3)

    def first(r, n):
        back = part3[0, pl.ds(r, n)] + part3[1, pl.ds(r + 1, n)] + part3[2, pl.ds(r + 2, n)]
        delta = back * slope_ref[pl.ds(r + 2, n)]
        padded[pl.ds(r + 2, n)] = delta[:, :, 0:128]
        col4[pl.ds(pl.multiple_of(r * Y, 16), n * Y), :] = stack_y(delta)

    over(130, first)
    padded[0:3] = jnp.zeros((3, Y, 128), F32)
    padded[131:134] = jnp.zeros((3, Y, 128), F32)

    def keep4(at, value):
        part4[at] = value

    dot_rows(nn, col4, b0_ref[...], keep4)

    def upper(z, n):
        back = (
            part4[pl.ds(z, n), :, 0:128]
            + part4[pl.ds(z + 1, n), :, 128:256]
            + part4[pl.ds(z + 2, n), :, 256:384]
        )
        value = keep_ref[pl.ds(z + 2, n)].astype(F32) * back
        du[pl.ds(z >> 1, n // 2)] = value.reshape(n // 2, 2, Y, 128)

    over(Z, upper)

    split = [du[:, e].reshape(K * Y, 128).astype(BF) for e in (0, 1)]
    row, lane = iota((K * Y, 128), 0), iota((K * Y, 128), 1)
    match = ((row & 1) == 0) == (lane < C)
    summed = nn(split[0], ud_ref[0]) + nn(split[1], ud_ref[1])
    summed = jnp.where(match, summed, 0.0).reshape(K, Y, 128)
    summed = summed + pltpu.roll(summed, Y - 1, 1)
    summed = summed + pltpu.roll(summed, C, 2)
    parent = summed.reshape(K * Y, 128).astype(BF)
    cell, src = iota((256, 512), 0), iota((256, 512), 1)
    pick = ones_where(src == (cell & (K - 1)) * Y + 2 * (cell >> 6))
    parent = nn(pick, parent)
    low = low_lanes(parent.shape)
    sides = [jnp.where(low, parent, 0.0), jnp.where(low, 0.0, parent)]
    slots = nn(hot_ref[...], jnp.concatenate(sides, axis=0).astype(BF))
    out_ref[:, 0:8, :] = slots.reshape(DEV, 8, 128).astype(BF)

    def put(index, block):
        out_ref[2 * index, 8:24, :] = block[0:16]
        out_ref[2 * index + 1, 8:24, :] = block[16:32]

    rec = rec_ref[...].astype(F32).reshape(K * Y, 128)
    rec = jnp.where(lane < C, rec, pltpu.roll(rec, C, 1))
    rec = jnp.where(match, rec, 0.0).astype(BF)
    for e in (0, 1):
        up_grad = tn(split[e], rec)
        for a in (0, 1):
            for b in (0, 1):
                block = up_grad[a * C : a * C + C, b * C : b * C + C]
                put(54 + 4 * a + 2 * b + e, packed(block))
    total[...] = wgrad(132, lambda *_: None, padded, shifted, lifted_col)
    tap_grads(total, lambda t, block: put(27 + t, block))
    for t in range(27):
        put(t, two_ref[t])
    out_ref[124:128, 8:24, :] = jnp.zeros((4, 16, 128), BF)


def sum_kernel(recv_ref, out_ref, *, scale):
    def one(i, total):
        return total + jnp.sum(recv_ref[pl.ds(i * 8, 8), 8:24, :].astype(F32), axis=0)

    total = lax.fori_loop(0, 16, one, jnp.zeros((16, 128), F32))
    out_ref[...] = jnp.broadcast_to((total * scale).astype(BF)[None], out_ref.shape)


def slot_kernel(recv_ref, out_ref):
    for chunk in range(16):
        block = recv_ref[chunk * 8 : chunk * 8 + 8, 0:8, :].astype(F32)
        halves = [block[:, None], pltpu.roll(block, C, 2)[:, None]]
        turned = jnp.concatenate(halves, axis=1).reshape(128, 128).T
        out_ref[0, :, chunk * 128 : chunk * 128 + 128] = turned[0:C].astype(BF)


def unpack_kernel(recv_ref, one_ref, two_ref, up_ref):
    def matrix(index):
        top = recv_ref[2 * index].astype(F32)
        low = recv_ref[2 * index + 1].astype(F32)
        both = jnp.concatenate([top, low], axis=0)
        return jnp.concatenate([both[:, :C], both[:, C:]], axis=0)

    for t in range(27):
        two_ref[t] = matrix(t)
        one_ref[t] = matrix(27 + t)
    for o in range(8):
        up_ref[o] = matrix(54 + o)


def shift(array, axis, step):
    count = lax.axis_size(axis)
    pairs = [(i, i + step) for i in range(count) if 0 <= i + step < count]
    return lax.ppermute(array, axis, pairs)


def exchange(array):
    return lax.all_to_all(array, ("gz", "xy"), 0, 0, tiled=True)


def local(
    parent_feat, parent_cell, send_count, up_weight, conv_one, conv_two, child_mask, cotangent
):
    size_x, size_y, size_z = cotangent.shape[1:]
    voxels = size_x * size_y * size_z * lax.axis_size("xy") * lax.axis_size("gz")
    scale = 1.0 / math.sqrt(voxels)
    sent = call(send_kernel, ((DEV, 16, 128), BF), raw=True, home=True, limit=58 << 20)(
        parent_feat, parent_cell, send_count
    )
    recv = exchange(sent)
    cot = cotangent.transpose(3, 2, 1, 0).reshape(Z, Y, 128)
    rec, up_edge, down_edge = call(
        grid_kernel, [((K, Y, 128), BF), ((4, Y, 128), BF), ((4, Y, 128), BF)]
    )(recv, child_mask, cot)
    before, after = shift(up_edge, "gz", 1), shift(down_edge, "gz", -1)
    rec_ext = jnp.concatenate([before[0:2], rec, after[0:2]], axis=0)
    left, right = shift(rec_ext, "xy", 1), shift(rec_ext, "xy", -1)
    weights = up_weight, conv_one, conv_two
    lift_own, seen_own, part_own, u, w1x, w2 = call(
        own_kernel,
        [
            ((KZ, 2, Y, 128), F32), ((KZ, 2, Y, 128), F32), ((3, 136, Y, 256), F32),
            ((768, 128), BF), ((3, 256, 768), BF), ((384, 768), BF),
        ],
        [((3, 256, 384), BF), ((1088, 384), BF)],
    )(rec_ext, *weights)
    act, delta, dec, slope, lifted, keep = call(
        forward_kernel,
        [
            ((134, Y, 256), BF), ((132, Y, 128), BF), ((132, Y, 128), BF),
            ((134, Y, 256), F32), ((136, Y, 256), BF), ((132, Y, 128), BF),
        ],
        [
            ((2, KZ, 2, Y, 128), F32), ((2, KZ, 2, Y, 128), F32), ((136, Y, 256), F32),
            ((1088, 768), BF), ((3, 136, Y, 256), F32), ((1072, 768), BF), ((134, Y, 384), F32),
            ((132, Y, 128), BF),
        ],
    )(left, right, before, after, cot, lift_own, seen_own, part_own, u, w1x, w2)
    delta_left, delta_right = shift(delta, "xy", 1), shift(delta, "xy", -1)
    two, hot, part_back, lifted_col, dec, b1x, b0, ud = call(
        second_grad_kernel,
        [
            ((27, 32, 128), BF), ((1024, 512), BF), ((3, 132, Y, 256), F32), ((1056, 768), BF),
            ((Z, Y, 128), BF), ((3, 768, 256), BF), ((768, 384), BF), ((2, 128, 128), BF),
        ],
        [
            ((3, 384, 256), BF), ((136, Y, 128), F32), ((1072, 384), BF), ((1072, 768), BF), ((384, 768), F32),
            ((1056, 384), BF),
        ],
        home=(False, False, False, False, True, False, False, False),
    )(act, delta, recv, lifted, dec, *weights)
    decoded = dec.reshape(Z, Y, 2, C).transpose(3, 2, 1, 0)
    message = call(
        backward_kernel,
        ((DEV, 24, 128), BF),
        [
            ((1056, 768), BF), ((3, 132, Y, 256), F32), ((1040, 768), BF), ((130, Y, 384), F32),
            ((134, Y, 128), F32), ((1056, 384), BF), ((384, 768), F32), ((K, 2, Y, 128), F32),
        ],
    )(
        delta_left, delta_right, slope, keep, rec, hot, part_back, lifted_col, two, b1x, b0, ud
    )
    back = exchange(message)
    total = call(functools.partial(sum_kernel, scale=scale), ((DEV, 16, 128), BF))(back)
    gathered = exchange(total)
    grad_parent = call(slot_kernel, ((1, C, 2048), BF), home=True)(back)
    grad_one, grad_two, grad_up = call(
        unpack_kernel, [((27, C, C), F32), ((27, C, C), F32), ((8, C, C), F32)], home=True
    )(gathered)
    return decoded, grad_parent, grad_one, grad_two, grad_up


def solution(mesh):
    placed = (
        P(("gz", "xy"), None, None),
        P(("gz", "xy"), None),
        P(("gz", "xy"), None),
        P(),
        P(),
        P(),
        P("xy", None, "gz"),
        P(None, "xy", None, "gz"),
    )
    return jax.shard_map(
        local,
        mesh=mesh,
        in_specs=placed,
        out_specs=(P(None, "xy", None, "gz"), P(("gz", "xy"), None, None), P(), P(), P()),
        check_vma=False,
    )
```

```python
import functools
import math

import jax
import jax.numpy as jnp
from jax import lax
from jax.experimental import pallas as pl
from jax.experimental.pallas import tpu as pltpu
from jax.sharding import PartitionSpec as P

BF = jnp.bfloat16
F32 = jnp.float32
XK = (0, 1, 2, -1, -2, 3)
C = 64
Z = 128
Y = 8
K = 64
KZ = K + 4
DEV = 128
NO_CELL = 256.0
ROWS = 10
STEP = 8


def iota(shape, dim):
    return lax.broadcasted_iota(jnp.int32, shape, dim)


def ones_where(cond):
    return jnp.where(cond, 1.0, 0.0).astype(BF)


def nt(a, b):
    return lax.dot_general(a, b, (((1,), (1,)), ((), ())), preferred_element_type=F32)


def nn(a, b):
    return lax.dot_general(a, b, (((1,), (0,)), ((), ())), preferred_element_type=F32)


def tn(a, b):
    return lax.dot_general(a, b, (((0,), (0,)), ((), ())), preferred_element_type=F32)


def over(total, body, step=STEP):
    full = total // step

    def one(i, carry):
        body(pl.multiple_of(i * step, step), step)
        return carry

    lax.fori_loop(0, full, one, 0)
    if total % step:
        body(full * step, total % step)


def low_lanes(shape):
    return iota(shape, len(shape) - 1) < C


def stack_y(block):
    count, rows, lanes = block.shape
    row = iota(block.shape, 1)
    below = jnp.where(row == 0, 0.0, pltpu.roll(block, 1, 1))
    above = jnp.where(row == rows - 1, 0.0, pltpu.roll(block, rows - 1, 1))
    wide = jnp.concatenate([below, block, above], axis=2)
    return wide.reshape(count * rows, 3 * lanes).astype(BF)


def call(kernel, outs, scratch=(), home=False, raw=False, limit=22 << 20):
    single = isinstance(outs, tuple)
    listed = [outs] if single else outs
    home = home if isinstance(home, tuple) else (home,) * len(listed)
    shapes = [
        jax.ShapeDtypeStruct(s, d) if h else pltpu.VMEM(s, d) for (s, d), h in zip(listed, home)
    ]
    vmem = pl.BlockSpec(memory_space=pltpu.VMEM)

    def run(*args):
        if not raw:
            args = [pltpu.with_memory_space_constraint(a, pltpu.VMEM) for a in args]
        got = pl.pallas_call(
            kernel,
            out_shape=shapes,
            in_specs=[vmem] * len(args),
            out_specs=[vmem] * len(shapes),
            scratch_shapes=[pltpu.VMEM(s, d) for s, d in scratch],
            compiler_params=pltpu.CompilerParams(vmem_limit_bytes=limit),
        )(*args)
        return got[0] if single else got

    return run


def dot_rows(dot, rows_ref, weights, put):
    total = rows_ref.shape[0]
    half = (total // 2 + 15) // 16 * 16
    for start, stop in ((0, half), (half, total)):
        got = dot(rows_ref[start:stop], weights)
        put(slice(start // Y, stop // Y), got.reshape((stop - start) // Y, Y, got.shape[1]))


def tap(ref, ox, oy, oz):
    if abs(ox) > 1:
        return jnp.zeros((C, C), BF)
    return ref[9 * (ox + 1) + 3 * (oy + 1) + oz + 1]


def join(a, b):
    return jnp.concatenate([a, b], axis=1)


def forward_weights(up_ref, one_ref, two_ref, w1o_ref, w1x_ref, w2_ref, u_ref):
    zero = jnp.zeros((C, C), BF)
    for oz in (-1, 0, 1):
        for oy in (-1, 0, 1):
            for n, xo in enumerate((0, 1, 2, -1)):
                rows = slice(n * C, n * C + C)
                for p in range(3):
                    ref, at = w1o_ref, (oy + 1) * 128
                    if p:
                        ref, at = w1x_ref, (oy + 1) * 256 + p * 128 - 128
                    pair = [tap(one_ref, XK[2 * p + s] - xo, oy, oz) for s in (0, 1)]
                    ref[oz + 1, rows, at : at + 128] = join(*pair)
            for n, xo in enumerate((0, 1)):
                at_row = (oz + 1) * 128 + n * C
                for p in range(2):
                    at = (oy + 1) * 256 + p * 128
                    pair = [tap(two_ref, XK[2 * p + s] - xo, oy, oz) for s in (0, 1)]
                    w2_ref[at_row : at_row + C, at : at + 128] = join(*pair)
    for e in (0, 1):
        for a in (0, 1):
            for b in (0, 1):
                at = (e * 4 + b * 2 + a) * C
                u_ref[at : at + C, :] = join(up_ref[4 * a + 2 * b + e], zero)
            at = 512 + (e * 2 + a) * C
            u_ref[at : at + C, :] = ones_where(iota((C, 128), 1) == C + 2 * a + e)


def backward_weights(up_ref, one_ref, two_ref, b1o_ref, b1x_ref, b0_ref, ud_ref):
    for oz in (-1, 0, 1):
        for oy in (-1, 0, 1):
            for kk, xk in enumerate(XK):
                ref, at_row = b1x_ref, (oy + 1) * 256 + kk * C - 128
                if kk < 2:
                    ref, at_row = b1o_ref, (oy + 1) * 128 + kk * C
                for p, pair in enumerate(((0, 1), (2, -1))):
                    ref[oz + 1, at_row : at_row + C, p * 128 : p * 128 + 128] = join(
                        *[tap(two_ref, xo - xk, -oy, -oz) for xo in pair]
                    )
            for kk, xk in enumerate(XK[:4]):
                at_row = (oy + 1) * 256 + kk * C
                at = (oz + 1) * 128
                b0_ref[at_row : at_row + C, at : at + 128] = join(
                    *[tap(one_ref, xo - xk, -oy, -oz) for xo in (0, 1)]
                )
    for e in (0, 1):
        for a in (0, 1):
            ud_ref[e, a * C : a * C + C, :] = join(up_ref[4 * a + e], up_ref[4 * a + 2 + e])


def send_kernel(feat_ref, cell_ref, count_ref, out_ref, rows_ref):
    counts = jnp.broadcast_to(count_ref[...].astype(F32), (DEV, DEV)).T
    lane = iota((8, 128), 1)
    for chunk in range(16):
        at = slice(chunk * 128, chunk * 128 + 128)
        feats = feat_ref[0, :, at].astype(F32)
        turned = jnp.concatenate([feats, feats], axis=0).T.reshape(8, 2, 8, 128)
        slots = jnp.where(low_lanes((8, 8, 128)), turned[:, 0], turned[:, 1])
        cells = jnp.broadcast_to(cell_ref[0:1, at].astype(F32), (8, 128))
        cells = pltpu.roll(cells, 0, 1, stride=16, stride_axis=0)
        cells = jnp.concatenate([cells[-d % 8 : -d % 8 + 1] for d in range(8)], axis=0)
        live = lane.astype(F32) < counts[chunk * 8 : chunk * 8 + 8]
        cells = jnp.where(live, cells, NO_CELL)
        for d in range(8):
            row = (chunk * 8 + d) * ROWS
            rows_ref[row : row + 8, :] = slots[d]
            rows_ref[row + 8 : row + 9, :] = cells[d : d + 1]
            rows_ref[row + 9 : row + 10, :] = cells[d : d + 1]
    out_ref[...] = rows_ref[...].astype(BF)


def equal(a, b):
    return jnp.where(a == b, jnp.ones((), BF), jnp.zeros((), BF))


def onehots(recv_ref, rows, wide_ref):
    count = DEV * rows
    lane = iota((1, count), 1)
    sender = lane // rows
    r = lane - sender * rows
    wide_ref[...] = recv_ref[...].astype(F32)
    cells = wide_ref[pl.ds(8, DEV, stride=ROWS), :].astype(BF)
    down = iota((DEV, count), 0)
    here = down == sender
    down = down.astype(F32).astype(BF)
    ids = iota((256, count), 0).astype(F32).astype(BF)
    hot = []
    for h in (0, 1):
        spot = jnp.where(r < 8, r + h * 8, 255).astype(F32).astype(BF)
        values = nn(cells, equal(down, spot))
        cell = jnp.sum(jnp.where(here, values, 0.0), axis=0, keepdims=True)
        cell = jnp.where(r < 8, cell, NO_CELL)
        hot.append(equal(ids, cell.astype(BF)))
    return hot


def grid_kernel(recv_ref, mask_ref, cot_ref, rec_ref, up_ref, down_ref, wide):
    first, second = [nn(hot, recv_ref[...]) for hot in onehots(recv_ref, ROWS, wide)]
    grid = jnp.where(low_lanes(first.shape), first + pltpu.roll(second, C, 1), 0.0).astype(BF)
    row, col = iota((512, 256), 0), iota((512, 256), 1)
    pick = ones_where(col == ((row & 7) >> 1) * K + (row >> 3))
    rec = nn(pick, grid)
    kk, zz = iota((K, Y, Z), 0), iota((K, Y, Z), 2)
    zrow, lane = iota((Z, 128), 0), iota((Z, 128), 1)
    for a in (0, 1):
        mine = jnp.where((zz >> 1) == kk, mask_ref[a].astype(F32)[None], 0.0)
        place = ones_where(lane == C + 2 * a + (zrow & 1))
        rec = rec + nn(mine.reshape(512, Z).astype(BF), place)
    rec = rec.reshape(K, Y, 128).astype(BF)
    rec_ref[...] = rec
    up_ref[0:2] = rec_ref[K - 2 : K]
    up_ref[2:4] = cot_ref[Z - 2 : Z]
    down_ref[0:2] = rec_ref[0:2]
    down_ref[2:4] = cot_ref[0:2]


def lane_groups(own, left, right):
    low = low_lanes(own.shape)
    return own, jnp.where(low, right, left), jnp.where(low, left, right)


def lift_tile(rec_ref, u_ref, lift, seen):
    kz = rec_ref.shape[0]
    rec = rec_ref[...].astype(F32).reshape(kz * Y, 128).astype(BF)
    odd_row = (iota((kz, Y, 128), 1) & 1) == 1
    for e in (0, 1):
        both = nt(rec, u_ref[e * 256 : e * 256 + 256, :]).reshape(kz, Y, 256)
        live = nt(rec, u_ref[512 + e * 128 : 640 + e * 128, :]).reshape(kz, Y, 128)
        lift[:, e] = live * jnp.where(odd_row, both[:, :, 128:], both[:, :, :128])
        seen[:, e] = live


def own_kernel(
    rec_ref, up_ref, one_ref, two_ref, lift, seen, part, u_ref, w1x_ref, w2_ref, w1o_ref, col
):
    forward_weights(up_ref, one_ref, two_ref, w1o_ref, w1x_ref, w2_ref, u_ref)
    lift_tile(rec_ref, u_ref, lift, seen)

    def columns(k0, n):
        own = lift[pl.ds(k0, n)].reshape(2 * n, Y, 128)
        col[pl.ds(pl.multiple_of(k0 * 16, 16), 16 * n), :] = stack_y(own)

    over(KZ, columns, 4)
    for s in range(3):

        def keep(at, value, s=s):
            part[s, at] = value

        dot_rows(nt, col, w1o_ref[s], keep)


def forward_kernel(
    left_ref, right_ref, before_ref, after_ref, cot_in_ref,
    lift_own, seen_own, part_own, u_ref, w1x_ref, w2_ref,
    act_ref, delta_ref, dec_ref, slope_ref, lifted_ref, keep_ref,
    lift, seen, mask, col1, part1, col2, part2, cot_ref,
):
    kz = KZ
    cot_ref[0:2] = before_ref[2:4]
    cot_ref[2 : 2 + Z] = cot_in_ref[...]
    cot_ref[2 + Z : 4 + Z] = after_ref[2:4]
    for t, ref in enumerate((left_ref, right_ref)):
        lift_tile(ref, u_ref, lift.at[t], seen.at[t])

    def columns(k0, n):
        def load(own_ref, ref):
            three = [own_ref[pl.ds(k0, n)], ref[0, pl.ds(k0, n)], ref[1, pl.ds(k0, n)]]
            return lane_groups(*[v.reshape(2 * n, Y, 128) for v in three])

        own, near, far = load(lift_own, lift)
        at = pl.ds(2 * k0, 2 * n)
        lifted_ref[at] = jnp.concatenate([own, near], axis=2).astype(BF)
        rows = pl.ds(pl.multiple_of(k0 * 16, 16), 16 * n)
        col1[rows, :] = stack_y(jnp.concatenate([near, far], axis=2))
        live_own, live_near, _ = load(seen_own, seen)
        mask[at] = jnp.concatenate([live_own, live_near], axis=2)

    over(kz, columns, 4)
    for s in range(3):

        def keep1(at, value, s=s):
            part1[s, at] = part_own[s, at] + value

        dot_rows(nt, col1, w1x_ref[s], keep1)

    def first(m, n):
        pre = part1[0, pl.ds(m, n)] + part1[1, pl.ds(m + 1, n)] + part1[2, pl.ds(m + 2, n)]
        live = mask[pl.ds(m + 1, n)]
        sig = jax.nn.sigmoid(pre)
        act = live * (pre * sig)
        slope_ref[pl.ds(m, n)] = live * (sig * (1.0 + pre * (1.0 - sig)))
        act_ref[pl.ds(m, n)] = act.astype(BF)
        col2[pl.ds(pl.multiple_of(m * Y, 16), n * Y), :] = stack_y(act)

    over(2 * kz - 2, first)

    def keep2(at, value):
        part2[at] = value

    dot_rows(nt, col2, w2_ref[...], keep2)

    def second(q, n):
        pre = (
            part2[pl.ds(q, n), :, 0:128]
            + part2[pl.ds(q + 1, n), :, 128:256]
            + part2[pl.ds(q + 2, n), :, 256:384]
        )
        live = mask[pl.ds(q + 2, n), :, 0:128]
        sig = jax.nn.sigmoid(pre)
        at = pl.ds(q, n)
        dec_ref[at] = (live * (pre * sig)).astype(BF)
        slope = live * (sig * (1.0 + pre * (1.0 - sig)))
        delta_ref[at] = (cot_ref[at].astype(F32) * slope).astype(BF)
        keep_ref[at] = live.astype(BF)

    over(2 * kz - 4, second)


def wgrad(count, padded, shifted, col, total):
    flat = padded[...].reshape((count + 2) * Y, 128).astype(BF).T
    width = count * Y
    for i, s in enumerate((2, 1, 0)):
        shifted[i * 128 : i * 128 + 128, :] = flat[:, s * Y : s * Y + width]
    for start in (0, 192):
        total[start : start + 192, :] = nn(shifted[start : start + 192, :], col[...])


def packed(block):
    return jnp.concatenate([block[0:32], block[32:64]], axis=1).astype(BF)


def tap_grads(total, put):
    place = {0: 0, 1: 1, 2: 2, -1: 3}
    for ox in (-1, 0, 1):
        for oy in (-1, 0, 1):
            for oz in (-1, 0, 1):
                sums = []
                for x in (0, 1):
                    r = (oz + 1) * 128 + x * C
                    c = (oy + 1) * 256 + place[x + ox] * C
                    sums.append(total[r : r + C, c : c + C])
                put(9 * (ox + 1) + 3 * (oy + 1) + oz + 1, packed(sums[0] + sums[1]))


def second_grad_kernel(
    act_ref, delta_ref, recv_ref, lifted_ref, dec_ref, rec_ref, up_ref, one_ref, two_ref,
    out_ref, hot_ref, part_ref, lifted_col, dec_out, b1x_ref, b0_ref, ud_ref, pick_ref, parent_ref,
    b1o_ref, padded, shifted, col, total, col3, wide,
):
    for h, hot in enumerate(onehots(recv_ref, 8, wide)):
        hot_ref[:, h * 256 : h * 256 + 256] = hot.T
    cell, src = iota((256, 512), 0), iota((256, 512), 1)
    pick_ref[...] = ones_where(src == (cell & (K - 1)) * Y + 2 * (cell >> 6))
    rec = rec_ref[...].astype(F32).reshape(K * Y, 128)
    row, lane = iota((K * Y, 128), 0), iota((K * Y, 128), 1)
    rec = jnp.where(lane < C, rec, pltpu.roll(rec, C, 1))
    parent_ref[...] = jnp.where(((row & 1) == 0) == (lane < C), rec, 0.0).astype(BF)
    dec_out[...] = dec_ref[2 : 2 + Z]
    backward_weights(up_ref, one_ref, two_ref, b1o_ref, b1x_ref, b0_ref, ud_ref)

    def columns(q, n):
        rows = pl.ds(pl.multiple_of(q * Y, 16), n * Y)
        col3[rows, :] = stack_y(delta_ref[pl.ds(q, n)].astype(F32))
        lifted_col[rows, :] = stack_y(lifted_ref[pl.ds(q + 2, n)].astype(F32))

    over(132, columns)
    for s in range(3):

        def keep(at, value, s=s):
            part_ref[s, at] = value

        dot_rows(nn, col3, b1o_ref[s], keep)
    padded[0:4] = jnp.zeros((4, Y, 128), F32)
    padded[132:136] = jnp.zeros((4, Y, 128), F32)
    padded[4:132] = delta_ref[2:130].astype(F32)
    def act_col(m, n):
        rows = pl.ds(pl.multiple_of(m * Y, 16), n * Y)
        col[rows, :] = stack_y(act_ref[pl.ds(m, n)].astype(F32))

    over(134, act_col)
    wgrad(134, padded, shifted, col, total)

    def put(t, block):
        out_ref[t] = block

    tap_grads(total, put)


def backward_kernel(
    left_ref, right_ref, slope_ref, keep_ref, hot_ref, part_own, lifted_col, two_ref,
    b1x_ref, b0_ref, ud_ref, pick_ref, parent_ref, out_ref,
    col3, part3, col4, part4, padded, shifted, total, du,
):
    def columns(q, n):
        at = pl.ds(q, n)
        left, right = left_ref[at].astype(F32), right_ref[at].astype(F32)
        groups = lane_groups(left, left, right)[1:]
        rows = pl.ds(pl.multiple_of(q * Y, 16), n * Y)
        col3[rows, :] = stack_y(jnp.concatenate(groups, axis=2))

    over(132, columns)
    for s in range(3):

        def keep3(at, value, s=s):
            part3[s, at] = part_own[s, at] + value

        dot_rows(nn, col3, b1x_ref[s], keep3)

    def first(r, n):
        back = part3[0, pl.ds(r, n)] + part3[1, pl.ds(r + 1, n)] + part3[2, pl.ds(r + 2, n)]
        delta = back * slope_ref[pl.ds(r + 2, n)]
        padded[pl.ds(r + 2, n)] = delta[:, :, 0:128]
        col4[pl.ds(pl.multiple_of(r * Y, 16), n * Y), :] = stack_y(delta)

    over(130, first)
    padded[0:3] = jnp.zeros((3, Y, 128), F32)
    padded[131:134] = jnp.zeros((3, Y, 128), F32)

    def keep4(at, value):
        part4[at] = value

    dot_rows(nn, col4, b0_ref[...], keep4)

    def upper(z, n):
        back = (
            part4[pl.ds(z, n), :, 0:128]
            + part4[pl.ds(z + 1, n), :, 128:256]
            + part4[pl.ds(z + 2, n), :, 256:384]
        )
        value = keep_ref[pl.ds(z + 2, n)].astype(F32) * back
        du[pl.ds(z >> 1, n // 2)] = value.reshape(n // 2, 2, Y, 128)

    over(Z, upper)

    split = [du[:, e].reshape(K * Y, 128).astype(BF) for e in (0, 1)]
    row, lane = iota((K * Y, 128), 0), iota((K * Y, 128), 1)
    match = ((row & 1) == 0) == (lane < C)
    summed = nn(split[0], ud_ref[0]) + nn(split[1], ud_ref[1])
    summed = jnp.where(match, summed, 0.0).reshape(K, Y, 128)
    summed = summed + pltpu.roll(summed, Y - 1, 1)
    summed = summed + pltpu.roll(summed, C, 2)
    parent = summed.reshape(K * Y, 128).astype(BF)
    parent = nn(pick_ref[...], parent)
    low = low_lanes(parent.shape)
    sides = [jnp.where(low, parent, 0.0), jnp.where(low, 0.0, parent)]
    slots = nn(hot_ref[...], jnp.concatenate(sides, axis=0).astype(BF))
    out_ref[:, 0:8, :] = slots.reshape(DEV, 8, 128).astype(BF)

    def put(index, block):
        out_ref[2 * index, 8:24, :] = block[0:16]
        out_ref[2 * index + 1, 8:24, :] = block[16:32]

    for e in (0, 1):
        up_grad = tn(split[e], parent_ref[...])
        for a in (0, 1):
            for b in (0, 1):
                block = up_grad[a * C : a * C + C, b * C : b * C + C]
                put(54 + 4 * a + 2 * b + e, packed(block))
    wgrad(132, padded, shifted, lifted_col, total)
    tap_grads(total, lambda t, block: put(27 + t, block))
    for t in range(27):
        put(t, two_ref[t])
    out_ref[124:128, 8:24, :] = jnp.zeros((4, 16, 128), BF)


def sum_kernel(recv_ref, out_ref, *, scale):
    def one(i, total):
        return total + jnp.sum(recv_ref[pl.ds(i * 8, 8), 8:24, :].astype(F32), axis=0)

    total = lax.fori_loop(0, 16, one, jnp.zeros((16, 128), F32))
    out_ref[...] = jnp.broadcast_to((total * scale).astype(BF)[None], out_ref.shape)


def slot_kernel(recv_ref, out_ref):
    for chunk in range(16):
        block = recv_ref[chunk * 8 : chunk * 8 + 8, 0:8, :].astype(F32)
        halves = [block[:, None], pltpu.roll(block, C, 2)[:, None]]
        turned = jnp.concatenate(halves, axis=1).reshape(128, 128).T
        out_ref[0, :, chunk * 128 : chunk * 128 + 128] = turned[0:C].astype(BF)


def unpack_kernel(recv_ref, one_ref, two_ref, up_ref):
    def matrix(index):
        top = recv_ref[2 * index].astype(F32)
        low = recv_ref[2 * index + 1].astype(F32)
        both = jnp.concatenate([top, low], axis=0)
        return jnp.concatenate([both[:, :C], both[:, C:]], axis=0)

    for t in range(27):
        two_ref[t] = matrix(t)
        one_ref[t] = matrix(27 + t)
    for o in range(8):
        up_ref[o] = matrix(54 + o)


def shift(array, axis, step):
    count = lax.axis_size(axis)
    pairs = [(i, i + step) for i in range(count) if 0 <= i + step < count]
    return lax.ppermute(array, axis, pairs)


def exchange(array):
    return lax.all_to_all(array, ("gz", "xy"), 0, 0, tiled=True)


def local(
    parent_feat, parent_cell, send_count, up_weight, conv_one, conv_two, child_mask, cotangent
):
    size_x, size_y, size_z = cotangent.shape[1:]
    voxels = size_x * size_y * size_z * lax.axis_size("xy") * lax.axis_size("gz")
    scale = 1.0 / math.sqrt(voxels)
    sent = call(send_kernel, ((DEV * ROWS, 128), BF), [((DEV * ROWS, 128), F32)], raw=True, limit=58 << 20)(
        parent_feat, parent_cell, send_count
    )
    recv = exchange(sent.reshape(DEV, ROWS // 2, 2, 128)).reshape(DEV * ROWS, 128)
    cot = cotangent.transpose(3, 2, 1, 0).reshape(Z, Y, 128)
    rec, up_edge, down_edge = call(
        grid_kernel,
        [((K, Y, 128), BF), ((4, Y, 128), BF), ((4, Y, 128), BF)],
        [((DEV * ROWS, 128), F32)],
    )(recv, child_mask, cot)
    before, after = shift(up_edge, "gz", 1), shift(down_edge, "gz", -1)
    rec_ext = jnp.concatenate([before[0:2], rec, after[0:2]], axis=0)
    left, right = shift(rec_ext, "xy", 1), shift(rec_ext, "xy", -1)
    weights = up_weight, conv_one, conv_two
    lift_own, seen_own, part_own, u, w1x, w2 = call(
        own_kernel,
        [
            ((KZ, 2, Y, 128), F32), ((KZ, 2, Y, 128), F32), ((3, 136, Y, 256), F32),
            ((768, 128), BF), ((3, 256, 768), BF), ((384, 768), BF),
        ],
        [((3, 256, 384), BF), ((1088, 384), BF)],
    )(rec_ext, *weights)
    act, delta, dec, slope, lifted, keep = call(
        forward_kernel,
        [
            ((134, Y, 256), BF), ((132, Y, 128), BF), ((132, Y, 128), BF),
            ((134, Y, 256), F32), ((136, Y, 256), BF), ((132, Y, 128), BF),
        ],
        [
            ((2, KZ, 2, Y, 128), F32), ((2, KZ, 2, Y, 128), F32), ((136, Y, 256), F32),
            ((1088, 768), BF), ((3, 136, Y, 256), F32), ((1072, 768), BF), ((134, Y, 384), F32),
            ((132, Y, 128), BF),
        ],
    )(left, right, before, after, cot, lift_own, seen_own, part_own, u, w1x, w2)
    delta_left, delta_right = shift(delta, "xy", 1), shift(delta, "xy", -1)
    two, hot, part_back, lifted_col, dec, b1x, b0, ud, pick, parent = call(
        second_grad_kernel,
        [
            ((27, 32, 128), BF), ((1024, 512), BF), ((3, 132, Y, 256), F32), ((1056, 768), BF),
            ((Z, Y, 128), BF), ((3, 768, 256), BF), ((768, 384), BF), ((2, 128, 128), BF),
            ((256, 512), BF), ((512, 128), BF),
        ],
        [
            ((3, 384, 256), BF), ((136, Y, 128), F32), ((384, 1072), BF), ((1072, 768), BF), ((384, 768), F32),
            ((1056, 384), BF), ((DEV * ROWS, 128), F32),
        ],
        home=(False, False, False, False, True, *[False] * 5),
    )(act, delta, recv, lifted, dec, rec, *weights)
    decoded = dec.reshape(Z, Y, 2, C).transpose(3, 2, 1, 0)
    message = call(
        backward_kernel,
        ((DEV, 24, 128), BF),
        [
            ((1056, 768), BF), ((3, 132, Y, 256), F32), ((1040, 768), BF), ((130, Y, 384), F32),
            ((134, Y, 128), F32), ((384, 1056), BF), ((384, 768), F32), ((K, 2, Y, 128), F32),
        ],
    )(
        delta_left, delta_right, slope, keep, hot, part_back, lifted_col, two, b1x, b0, ud, pick, parent
    )
    back = exchange(message)
    total = call(functools.partial(sum_kernel, scale=scale), ((DEV, 16, 128), BF))(back)
    gathered = exchange(total)
    grad_parent = call(slot_kernel, ((1, C, 2048), BF), home=True)(back)
    grad_one, grad_two, grad_up = call(
        unpack_kernel, [((27, C, C), F32), ((27, C, C), F32), ((8, C, C), F32)], home=True
    )(gathered)
    return decoded, grad_parent, grad_one, grad_two, grad_up


def solution(mesh):
    placed = (
        P(("gz", "xy"), None, None),
        P(("gz", "xy"), None),
        P(("gz", "xy"), None),
        P(),
        P(),
        P(),
        P("xy", None, "gz"),
        P(None, "xy", None, "gz"),
    )
    return jax.shard_map(
        local,
        mesh=mesh,
        in_specs=placed,
        out_specs=(P(None, "xy", None, "gz"), P(("gz", "xy"), None, None), P(), P(), P()),
        check_vma=False,
    )
```

```python
import functools
import math

import jax
import jax.numpy as jnp
from jax import lax
from jax.experimental import pallas as pl
from jax.experimental.pallas import tpu as pltpu
from jax.sharding import PartitionSpec as P

BF = jnp.bfloat16
F32 = jnp.float32
XK = (0, 1, 2, -1, -2, 3)
C = 64
Z = 128
Y = 8
K = 64
KZ = K + 4
DEV = 128
NO_CELL = 256.0
ROWS = 10
STEP = 8


def iota(shape, dim):
    return lax.broadcasted_iota(jnp.int32, shape, dim)


def ones_where(cond):
    return jnp.where(cond, 1.0, 0.0).astype(BF)


def nt(a, b):
    return lax.dot_general(a, b, (((1,), (1,)), ((), ())), preferred_element_type=F32)


def nn(a, b):
    return lax.dot_general(a, b, (((1,), (0,)), ((), ())), preferred_element_type=F32)


def tn(a, b):
    return lax.dot_general(a, b, (((0,), (0,)), ((), ())), preferred_element_type=F32)


def over(total, body, step=STEP):
    full = total // step

    def one(i, carry):
        body(pl.multiple_of(i * step, step), step)
        return carry

    lax.fori_loop(0, full, one, 0)
    if total % step:
        body(full * step, total % step)


def low_lanes(shape):
    return iota(shape, len(shape) - 1) < C


def stack_y(block):
    count, rows, lanes = block.shape
    row = iota(block.shape, 1)
    below = jnp.where(row == 0, 0.0, pltpu.roll(block, 1, 1))
    above = jnp.where(row == rows - 1, 0.0, pltpu.roll(block, rows - 1, 1))
    wide = jnp.concatenate([below, block, above], axis=2)
    return wide.reshape(count * rows, 3 * lanes).astype(BF)


def call(kernel, outs, scratch=(), home=False, raw=False, limit=22 << 20):
    single = isinstance(outs, tuple)
    listed = [outs] if single else outs
    home = home if isinstance(home, tuple) else (home,) * len(listed)
    shapes = [
        jax.ShapeDtypeStruct(s, d) if h else pltpu.VMEM(s, d) for (s, d), h in zip(listed, home)
    ]
    vmem = pl.BlockSpec(memory_space=pltpu.VMEM)

    def run(*args):
        if not raw:
            args = [pltpu.with_memory_space_constraint(a, pltpu.VMEM) for a in args]
        got = pl.pallas_call(
            kernel,
            out_shape=shapes,
            in_specs=[vmem] * len(args),
            out_specs=[vmem] * len(shapes),
            scratch_shapes=[pltpu.VMEM(s, d) for s, d in scratch],
            compiler_params=pltpu.CompilerParams(vmem_limit_bytes=limit),
        )(*args)
        return got[0] if single else got

    return run


def dot_rows(dot, rows_ref, weights, put):
    total = rows_ref.shape[0]
    half = (total // 2 + 15) // 16 * 16
    for start, stop in ((0, half), (half, total)):
        got = dot(rows_ref[start:stop], weights)
        put(slice(start // Y, stop // Y), got.reshape((stop - start) // Y, Y, got.shape[1]))


def tap(ref, ox, oy, oz):
    if abs(ox) > 1:
        return jnp.zeros((C, C), BF)
    return ref[9 * (ox + 1) + 3 * (oy + 1) + oz + 1]


def join(a, b):
    return jnp.concatenate([a, b], axis=1)


def forward_weights(up_ref, one_ref, two_ref, w1o_ref, w1x_ref, w2_ref, u_ref):
    zero = jnp.zeros((C, C), BF)
    for oz in (-1, 0, 1):
        for oy in (-1, 0, 1):
            for n, xo in enumerate((0, 1, 2, -1)):
                rows = slice(n * C, n * C + C)
                for p in range(3):
                    ref, at = w1o_ref, (oy + 1) * 128
                    if p:
                        ref, at = w1x_ref, (oy + 1) * 256 + p * 128 - 128
                    pair = [tap(one_ref, XK[2 * p + s] - xo, oy, oz) for s in (0, 1)]
                    ref[oz + 1, rows, at : at + 128] = join(*pair)
            for n, xo in enumerate((0, 1)):
                at_row = (oz + 1) * 128 + n * C
                for p in range(2):
                    at = (oy + 1) * 256 + p * 128
                    pair = [tap(two_ref, XK[2 * p + s] - xo, oy, oz) for s in (0, 1)]
                    w2_ref[at_row : at_row + C, at : at + 128] = join(*pair)
    for e in (0, 1):
        for a in (0, 1):
            for b in (0, 1):
                at = (e * 4 + b * 2 + a) * C
                u_ref[at : at + C, :] = join(up_ref[4 * a + 2 * b + e], zero)
            at = 512 + (e * 2 + a) * C
            u_ref[at : at + C, :] = ones_where(iota((C, 128), 1) == C + 2 * a + e)


def backward_weights(up_ref, one_ref, two_ref, b1o_ref, b1x_ref, b0_ref, ud_ref):
    for oz in (-1, 0, 1):
        for oy in (-1, 0, 1):
            for kk, xk in enumerate(XK):
                ref, at_row = b1x_ref, (oy + 1) * 256 + kk * C - 128
                if kk < 2:
                    ref, at_row = b1o_ref, (oy + 1) * 128 + kk * C
                for p, pair in enumerate(((0, 1), (2, -1))):
                    ref[oz + 1, at_row : at_row + C, p * 128 : p * 128 + 128] = join(
                        *[tap(two_ref, xo - xk, -oy, -oz) for xo in pair]
                    )
            for kk, xk in enumerate(XK[:4]):
                at_row = (oy + 1) * 256 + kk * C
                at = (oz + 1) * 128
                b0_ref[at_row : at_row + C, at : at + 128] = join(
                    *[tap(one_ref, xo - xk, -oy, -oz) for xo in (0, 1)]
                )
    for e in (0, 1):
        for a in (0, 1):
            ud_ref[e, a * C : a * C + C, :] = join(up_ref[4 * a + e], up_ref[4 * a + 2 + e])


def send_kernel(feat_ref, cell_ref, count_ref, out_ref, rows_ref):
    counts = jnp.broadcast_to(count_ref[...].astype(F32), (DEV, DEV)).T
    lane = iota((8, 128), 1)
    for chunk in range(16):
        at = slice(chunk * 128, chunk * 128 + 128)
        feats = feat_ref[0, :, at].astype(F32)
        turned = jnp.concatenate([feats, feats], axis=0).T.reshape(8, 2, 8, 128)
        slots = jnp.where(low_lanes((8, 8, 128)), turned[:, 0], turned[:, 1])
        cells = jnp.broadcast_to(cell_ref[0:1, at].astype(F32), (8, 128))
        cells = pltpu.roll(cells, 0, 1, stride=16, stride_axis=0)
        cells = jnp.concatenate([cells[-d % 8 : -d % 8 + 1] for d in range(8)], axis=0)
        live = lane.astype(F32) < counts[chunk * 8 : chunk * 8 + 8]
        cells = jnp.where(live, cells, NO_CELL)
        for d in range(8):
            row = (chunk * 8 + d) * ROWS
            rows_ref[row : row + 8, :] = slots[d]
            rows_ref[row + 8 : row + 9, :] = cells[d : d + 1]
            rows_ref[row + 9 : row + 10, :] = cells[d : d + 1]
    out_ref[...] = rows_ref[...].astype(BF)


def equal(a, b):
    return jnp.where(a == b, jnp.ones((), BF), jnp.zeros((), BF))


def onehots(recv_ref, rows, wide_ref):
    count = DEV * rows
    lane = iota((1, count), 1)
    sender = lane // rows
    r = lane - sender * rows
    wide_ref[...] = recv_ref[...].astype(F32)
    cells = wide_ref[pl.ds(8, DEV, stride=ROWS), :].astype(BF)
    down = iota((DEV, count), 0)
    here = down == sender
    down = down.astype(F32).astype(BF)
    ids = iota((256, count), 0).astype(F32).astype(BF)
    hot = []
    for h in (0, 1):
        spot = jnp.where(r < 8, r + h * 8, 255).astype(F32).astype(BF)
        values = nn(cells, equal(down, spot))
        cell = jnp.sum(jnp.where(here, values, 0.0), axis=0, keepdims=True)
        cell = jnp.where(r < 8, cell, NO_CELL)
        hot.append(equal(ids, cell.astype(BF)))
    return hot


def grid_kernel(recv_ref, mask_ref, cot_ref, rec_ref, up_ref, down_ref, wide):
    first, second = [nn(hot, recv_ref[...]) for hot in onehots(recv_ref, ROWS, wide)]
    grid = jnp.where(low_lanes(first.shape), first + pltpu.roll(second, C, 1), 0.0).astype(BF)
    row, col = iota((512, 256), 0), iota((512, 256), 1)
    pick = ones_where(col == ((row & 7) >> 1) * K + (row >> 3))
    rec = nn(pick, grid)
    kk, zz = iota((K, Y, Z), 0), iota((K, Y, Z), 2)
    zrow, lane = iota((Z, 128), 0), iota((Z, 128), 1)
    for a in (0, 1):
        mine = jnp.where((zz >> 1) == kk, mask_ref[a].astype(F32)[None], 0.0)
        place = ones_where(lane == C + 2 * a + (zrow & 1))
        rec = rec + nn(mine.reshape(512, Z).astype(BF), place)
    rec = rec.reshape(K, Y, 128).astype(BF)
    rec_ref[...] = rec
    up_ref[0:2] = rec_ref[K - 2 : K]
    up_ref[2:4] = cot_ref[Z - 2 : Z]
    down_ref[0:2] = rec_ref[0:2]
    down_ref[2:4] = cot_ref[0:2]


def side_groups(side, far_pair, near_pair):
    low = jnp.broadcast_to(side[None], near_pair.shape)
    return jnp.where(low, near_pair, far_pair), jnp.where(low, far_pair, near_pair)


def lift_tile(rec_ref, u_ref, lift, seen):
    kz = rec_ref.shape[0]
    rec = rec_ref[...].astype(F32).reshape(kz * Y, 128).astype(BF)
    odd_row = (iota((kz, Y, 128), 1) & 1) == 1
    for e in (0, 1):
        both = nt(rec, u_ref[e * 256 : e * 256 + 256, :]).reshape(kz, Y, 256)
        live = nt(rec, u_ref[512 + e * 128 : 640 + e * 128, :]).reshape(kz, Y, 128)
        lift[:, e] = live * jnp.where(odd_row, both[:, :, 128:], both[:, :, :128])
        seen[:, e] = live


def own_kernel(
    rec_ref, up_ref, one_ref, two_ref, lift, seen, part, u_ref, w1x_ref, w2_ref, w1o_ref, col
):
    forward_weights(up_ref, one_ref, two_ref, w1o_ref, w1x_ref, w2_ref, u_ref)
    lift_tile(rec_ref, u_ref, lift, seen)

    def columns(k0, n):
        own = lift[pl.ds(k0, n)].reshape(2 * n, Y, 128)
        col[pl.ds(pl.multiple_of(k0 * 16, 16), 16 * n), :] = stack_y(own)

    over(KZ, columns, 4)
    for s in range(3):

        def keep(at, value, s=s):
            part[s, at] = value

        dot_rows(nt, col, w1o_ref[s], keep)


def forward_kernel(
    far_ref, near_ref, side_ref, cot_ref,
    lift_own, seen_own, part_own, u_ref, w1x_ref, w2_ref,
    act_ref, delta_ref, dec_ref, slope_ref, lifted_ref, keep_ref,
    lift, seen, mask, col1, part1, col2, part2,
):
    kz = KZ
    side = side_ref[...] != 0
    for t, ref in enumerate((far_ref, near_ref)):
        lift_tile(ref, u_ref, lift.at[t], seen.at[t])

    def columns(k0, n):
        def load(own_ref, ref):
            three = [own_ref[pl.ds(k0, n)], ref[0, pl.ds(k0, n)], ref[1, pl.ds(k0, n)]]
            three = [v.reshape(2 * n, Y, 128) for v in three]
            return three[0], *side_groups(side, *three[1:])

        own, near, far = load(lift_own, lift)
        at = pl.ds(2 * k0, 2 * n)
        lifted_ref[at] = jnp.concatenate([own, near], axis=2).astype(BF)
        rows = pl.ds(pl.multiple_of(k0 * 16, 16), 16 * n)
        col1[rows, :] = stack_y(jnp.concatenate([near, far], axis=2))
        live_own, live_near, _ = load(seen_own, seen)
        mask[at] = jnp.concatenate([live_own, live_near], axis=2)

    over(kz, columns, 4)
    for s in range(3):

        def keep1(at, value, s=s):
            part1[s, at] = part_own[s, at] + value

        dot_rows(nt, col1, w1x_ref[s], keep1)

    def first(m, n):
        pre = part1[0, pl.ds(m, n)] + part1[1, pl.ds(m + 1, n)] + part1[2, pl.ds(m + 2, n)]
        live = mask[pl.ds(m + 1, n)]
        sig = jax.nn.sigmoid(pre)
        act = live * (pre * sig)
        slope_ref[pl.ds(m, n)] = live * (sig * (1.0 + pre * (1.0 - sig)))
        act_ref[pl.ds(m, n)] = act.astype(BF)
        col2[pl.ds(pl.multiple_of(m * Y, 16), n * Y), :] = stack_y(act)

    over(2 * kz - 2, first)

    def keep2(at, value):
        part2[at] = value

    dot_rows(nt, col2, w2_ref[...], keep2)

    def second(q, n):
        pre = (
            part2[pl.ds(q, n), :, 0:128]
            + part2[pl.ds(q + 1, n), :, 128:256]
            + part2[pl.ds(q + 2, n), :, 256:384]
        )
        live = mask[pl.ds(q + 2, n), :, 0:128]
        sig = jax.nn.sigmoid(pre)
        at = pl.ds(q, n)
        dec_ref[at] = (live * (pre * sig)).astype(BF)
        slope = live * (sig * (1.0 + pre * (1.0 - sig)))
        delta_ref[at] = (cot_ref[at].astype(F32) * slope).astype(BF)
        keep_ref[at] = live.astype(BF)

    over(2 * kz - 4, second)


def wgrad(count, padded, shifted, col, total):
    flat = padded[...].reshape((count + 2) * Y, 128).astype(BF).T
    width = count * Y
    for i, s in enumerate((2, 1, 0)):
        shifted[i * 128 : i * 128 + 128, :] = flat[:, s * Y : s * Y + width]
    for start in (0, 192):
        total[start : start + 192, :] = nn(shifted[start : start + 192, :], col[...])


def packed(block):
    return jnp.concatenate([block[0:32], block[32:64]], axis=1).astype(BF)


def tap_grads(total, put):
    place = {0: 0, 1: 1, 2: 2, -1: 3}
    for ox in (-1, 0, 1):
        for oy in (-1, 0, 1):
            for oz in (-1, 0, 1):
                sums = []
                for x in (0, 1):
                    r = (oz + 1) * 128 + x * C
                    c = (oy + 1) * 256 + place[x + ox] * C
                    sums.append(total[r : r + C, c : c + C])
                put(9 * (ox + 1) + 3 * (oy + 1) + oz + 1, packed(sums[0] + sums[1]))


def second_grad_kernel(
    act_ref, delta_ref, recv_ref, lifted_ref, dec_ref, rec_ref, up_ref, one_ref, two_ref,
    out_ref, hot_ref, part_ref, lifted_col, dec_out, b1x_ref, b0_ref, ud_ref, pick_ref, parent_ref,
    b1o_ref, padded, shifted, col, total, col3, wide,
):
    for h, hot in enumerate(onehots(recv_ref, 8, wide)):
        hot_ref[:, h * 256 : h * 256 + 256] = hot.T
    cell, src = iota((256, 512), 0), iota((256, 512), 1)
    pick_ref[...] = ones_where(src == (cell & (K - 1)) * Y + 2 * (cell >> 6))
    rec = rec_ref[...].astype(F32).reshape(K * Y, 128)
    row, lane = iota((K * Y, 128), 0), iota((K * Y, 128), 1)
    rec = jnp.where(lane < C, rec, pltpu.roll(rec, C, 1))
    parent_ref[...] = jnp.where(((row & 1) == 0) == (lane < C), rec, 0.0).astype(BF)
    dec_out[...] = dec_ref[2 : 2 + Z]
    backward_weights(up_ref, one_ref, two_ref, b1o_ref, b1x_ref, b0_ref, ud_ref)

    def columns(q, n):
        rows = pl.ds(pl.multiple_of(q * Y, 16), n * Y)
        col3[rows, :] = stack_y(delta_ref[pl.ds(q, n)].astype(F32))
        lifted_col[rows, :] = stack_y(lifted_ref[pl.ds(q + 2, n)].astype(F32))

    over(132, columns)
    for s in range(3):

        def keep(at, value, s=s):
            part_ref[s, at] = value

        dot_rows(nn, col3, b1o_ref[s], keep)
    padded[0:4] = jnp.zeros((4, Y, 128), F32)
    padded[132:136] = jnp.zeros((4, Y, 128), F32)
    padded[4:132] = delta_ref[2:130].astype(F32)
    def act_col(m, n):
        rows = pl.ds(pl.multiple_of(m * Y, 16), n * Y)
        col[rows, :] = stack_y(act_ref[pl.ds(m, n)].astype(F32))

    over(134, act_col)
    wgrad(134, padded, shifted, col, total)

    def put(t, block):
        out_ref[t] = block

    tap_grads(total, put)


def backward_kernel(
    far_ref, near_ref, side_ref, slope_ref, keep_ref, hot_ref, part_own, lifted_col, two_ref,
    b1x_ref, b0_ref, ud_ref, pick_ref, parent_ref, out_ref,
    col3, part3, col4, part4, padded, shifted, total, du,
):
    side = side_ref[...] != 0

    def columns(q, n):
        at = pl.ds(q, n)
        groups = side_groups(side, far_ref[at].astype(F32), near_ref[at].astype(F32))
        rows = pl.ds(pl.multiple_of(q * Y, 16), n * Y)
        col3[rows, :] = stack_y(jnp.concatenate(groups, axis=2))

    over(132, columns)
    for s in range(3):

        def keep3(at, value, s=s):
            part3[s, at] = part_own[s, at] + value

        dot_rows(nn, col3, b1x_ref[s], keep3)

    def first(r, n):
        back = part3[0, pl.ds(r, n)] + part3[1, pl.ds(r + 1, n)] + part3[2, pl.ds(r + 2, n)]
        delta = back * slope_ref[pl.ds(r + 2, n)]
        padded[pl.ds(r + 2, n)] = delta[:, :, 0:128]
        col4[pl.ds(pl.multiple_of(r * Y, 16), n * Y), :] = stack_y(delta)

    over(130, first)
    padded[0:3] = jnp.zeros((3, Y, 128), F32)
    padded[131:134] = jnp.zeros((3, Y, 128), F32)

    def keep4(at, value):
        part4[at] = value

    dot_rows(nn, col4, b0_ref[...], keep4)

    def upper(z, n):
        back = (
            part4[pl.ds(z, n), :, 0:128]
            + part4[pl.ds(z + 1, n), :, 128:256]
            + part4[pl.ds(z + 2, n), :, 256:384]
        )
        value = keep_ref[pl.ds(z + 2, n)].astype(F32) * back
        du[pl.ds(z >> 1, n // 2)] = value.reshape(n // 2, 2, Y, 128)

    over(Z, upper)

    split = [du[:, e].reshape(K * Y, 128).astype(BF) for e in (0, 1)]
    row, lane = iota((K * Y, 128), 0), iota((K * Y, 128), 1)
    match = ((row & 1) == 0) == (lane < C)
    summed = nn(split[0], ud_ref[0]) + nn(split[1], ud_ref[1])
    summed = jnp.where(match, summed, 0.0).reshape(K, Y, 128)
    summed = summed + pltpu.roll(summed, Y - 1, 1)
    summed = summed + pltpu.roll(summed, C, 2)
    parent = summed.reshape(K * Y, 128).astype(BF)
    parent = nn(pick_ref[...], parent)
    low = low_lanes(parent.shape)
    sides = [jnp.where(low, parent, 0.0), jnp.where(low, 0.0, parent)]
    slots = nn(hot_ref[...], jnp.concatenate(sides, axis=0).astype(BF))
    out_ref[:, 0:8, :] = slots.reshape(DEV, 8, 128).astype(BF)

    def put(index, block):
        out_ref[2 * index, 8:24, :] = block[0:16]
        out_ref[2 * index + 1, 8:24, :] = block[16:32]

    for e in (0, 1):
        up_grad = tn(split[e], parent_ref[...])
        for a in (0, 1):
            for b in (0, 1):
                block = up_grad[a * C : a * C + C, b * C : b * C + C]
                put(54 + 4 * a + 2 * b + e, packed(block))
    wgrad(132, padded, shifted, lifted_col, total)
    tap_grads(total, lambda t, block: put(27 + t, block))
    for t in range(27):
        put(t, two_ref[t])
    out_ref[124:128, 8:24, :] = jnp.zeros((4, 16, 128), BF)


def sum_kernel(recv_ref, out_ref, *, scale):
    def one(i, total):
        return total + jnp.sum(recv_ref[pl.ds(i * 8, 8), 8:24, :].astype(F32), axis=0)

    total = lax.fori_loop(0, 16, one, jnp.zeros((16, 128), F32))
    out_ref[...] = jnp.broadcast_to((total * scale).astype(BF)[None], out_ref.shape)


def slot_kernel(recv_ref, out_ref):
    for chunk in range(16):
        block = recv_ref[chunk * 8 : chunk * 8 + 8, 0:8, :].astype(F32)
        halves = [block[:, None], pltpu.roll(block, C, 2)[:, None]]
        turned = jnp.concatenate(halves, axis=1).reshape(128, 128).T
        out_ref[0, :, chunk * 128 : chunk * 128 + 128] = turned[0:C].astype(BF)


def unpack_kernel(recv_ref, one_ref, two_ref, up_ref):
    def matrix(index):
        top = recv_ref[2 * index].astype(F32)
        low = recv_ref[2 * index + 1].astype(F32)
        both = jnp.concatenate([top, low], axis=0)
        return jnp.concatenate([both[:, :C], both[:, C:]], axis=0)

    for t in range(27):
        two_ref[t] = matrix(t)
        one_ref[t] = matrix(27 + t)
    for o in range(8):
        up_ref[o] = matrix(54 + o)


def swap(array, axis, first):
    count = lax.axis_size(axis)
    pairs = [(i, i + 1) for i in range(first, count - 1, 2)]
    return lax.ppermute(array, axis, pairs + [(j, i) for i, j in pairs])


def swaps(far, near, axis):
    return swap(far, axis, 1), swap(near, axis, 0)


def exchange(array):
    return lax.all_to_all(array, ("gz", "xy"), 0, 0, tiled=True)


def local(
    parent_feat, parent_cell, send_count, up_weight, conv_one, conv_two, child_mask, cotangent
):
    size_x, size_y, size_z = cotangent.shape[1:]
    voxels = size_x * size_y * size_z * lax.axis_size("xy") * lax.axis_size("gz")
    scale = 1.0 / math.sqrt(voxels)
    sent = call(send_kernel, ((DEV * ROWS, 128), BF), [((DEV * ROWS, 128), F32)], raw=True, limit=58 << 20)(
        parent_feat, parent_cell, send_count
    )
    recv = exchange(sent.reshape(DEV, ROWS // 2, 2, 128)).reshape(DEV * ROWS, 128)
    cot = cotangent.transpose(3, 2, 1, 0).reshape(Z, Y, 128)
    rec, up_edge, down_edge = call(
        grid_kernel,
        [((K, Y, 128), BF), ((4, Y, 128), BF), ((4, Y, 128), BF)],
        [((DEV * ROWS, 128), F32)],
    )(recv, child_mask, cot)
    odd_z = lax.axis_index("gz") % 2 == 1
    far, near = swaps(
        jnp.where(odd_z, up_edge, down_edge), jnp.where(odd_z, down_edge, up_edge), "gz"
    )
    before, after = jnp.where(odd_z, near, far), jnp.where(odd_z, far, near)
    rec_ext = jnp.concatenate([before[0:2], rec, after[0:2]], axis=0)
    cot_ext = jnp.concatenate([before[2:4], cot, after[2:4]], axis=0)
    even_x = lax.axis_index("xy") % 2 == 0
    side = (low_lanes((8, 128)) == even_x).astype(jnp.int32)
    rec_far, rec_near = swaps(rec_ext, rec_ext, "xy")
    weights = up_weight, conv_one, conv_two
    lift_own, seen_own, part_own, u, w1x, w2 = call(
        own_kernel,
        [
            ((KZ, 2, Y, 128), F32), ((KZ, 2, Y, 128), F32), ((3, 136, Y, 256), F32),
            ((768, 128), BF), ((3, 256, 768), BF), ((384, 768), BF),
        ],
        [((3, 256, 384), BF), ((1088, 384), BF)],
    )(rec_ext, *weights)
    act, delta, dec, slope, lifted, keep = call(
        forward_kernel,
        [
            ((134, Y, 256), BF), ((132, Y, 128), BF), ((132, Y, 128), BF),
            ((134, Y, 256), F32), ((136, Y, 256), BF), ((132, Y, 128), BF),
        ],
        [
            ((2, KZ, 2, Y, 128), F32), ((2, KZ, 2, Y, 128), F32), ((136, Y, 256), F32),
            ((1088, 768), BF), ((3, 136, Y, 256), F32), ((1072, 768), BF), ((134, Y, 384), F32),
        ],
    )(rec_far, rec_near, side, cot_ext, lift_own, seen_own, part_own, u, w1x, w2)
    delta_far, delta_near = swaps(delta, delta, "xy")
    two, hot, part_back, lifted_col, dec, b1x, b0, ud, pick, parent = call(
        second_grad_kernel,
        [
            ((27, 32, 128), BF), ((1024, 512), BF), ((3, 132, Y, 256), F32), ((1056, 768), BF),
            ((Z, Y, 128), BF), ((3, 768, 256), BF), ((768, 384), BF), ((2, 128, 128), BF),
            ((256, 512), BF), ((512, 128), BF),
        ],
        [
            ((3, 384, 256), BF), ((136, Y, 128), F32), ((384, 1072), BF), ((1072, 768), BF), ((384, 768), F32),
            ((1056, 384), BF), ((DEV * ROWS, 128), F32),
        ],
        home=(False, False, False, False, True, *[False] * 5),
    )(act, delta, recv, lifted, dec, rec, *weights)
    decoded = dec.reshape(Z, Y, 2, C).transpose(3, 2, 1, 0)
    message = call(
        backward_kernel,
        ((DEV, 24, 128), BF),
        [
            ((1056, 768), BF), ((3, 132, Y, 256), F32), ((1040, 768), BF), ((130, Y, 384), F32),
            ((134, Y, 128), F32), ((384, 1056), BF), ((384, 768), F32), ((K, 2, Y, 128), F32),
        ],
    )(
        delta_far, delta_near, side, slope, keep, hot, part_back, lifted_col, two, b1x, b0, ud, pick, parent
    )
    back = exchange(message)
    total = call(functools.partial(sum_kernel, scale=scale), ((DEV, 16, 128), BF))(back)
    gathered = exchange(total)
    grad_parent = call(slot_kernel, ((1, C, 2048), BF), home=True)(back)
    grad_one, grad_two, grad_up = call(
        unpack_kernel, [((27, C, C), F32), ((27, C, C), F32), ((8, C, C), F32)], home=True
    )(gathered)
    return decoded, grad_parent, grad_one, grad_two, grad_up


def solution(mesh):
    placed = (
        P(("gz", "xy"), None, None),
        P(("gz", "xy"), None),
        P(("gz", "xy"), None),
        P(),
        P(),
        P(),
        P("xy", None, "gz"),
        P(None, "xy", None, "gz"),
    )
    return jax.shard_map(
        local,
        mesh=mesh,
        in_specs=placed,
        out_specs=(P(None, "xy", None, "gz"), P(("gz", "xy"), None, None), P(), P(), P()),
        check_vma=False,
    )
```

```python
import functools
import math

import jax
import jax.numpy as jnp
from jax import lax
from jax.experimental import pallas as pl
from jax.experimental.pallas import tpu as pltpu
from jax.sharding import PartitionSpec as P

BF = jnp.bfloat16
F32 = jnp.float32
XK = (0, 1, 2, -1, -2, 3)
C = 64
Z = 128
Y = 8
K = 64
KZ = K + 4
DEV = 128
NO_CELL = 256.0
ROWS = 10
STEP = 8


def iota(shape, dim):
    return lax.broadcasted_iota(jnp.int32, shape, dim)


def ones_where(cond):
    return jnp.where(cond, 1.0, 0.0).astype(BF)


def nt(a, b):
    return lax.dot_general(a, b, (((1,), (1,)), ((), ())), preferred_element_type=F32)


def nn(a, b):
    return lax.dot_general(a, b, (((1,), (0,)), ((), ())), preferred_element_type=F32)


def tn(a, b):
    return lax.dot_general(a, b, (((0,), (0,)), ((), ())), preferred_element_type=F32)


def over(total, body, step=STEP):
    full = total // step

    def one(i, carry):
        body(pl.multiple_of(i * step, step), step)
        return carry

    lax.fori_loop(0, full, one, 0)
    if total % step:
        body(full * step, total % step)


def low_lanes(shape):
    return iota(shape, len(shape) - 1) < C


def stack_y(block):
    count, rows, lanes = block.shape
    row = iota(block.shape, 1)
    below = jnp.where(row == 0, 0.0, pltpu.roll(block, 1, 1))
    above = jnp.where(row == rows - 1, 0.0, pltpu.roll(block, rows - 1, 1))
    wide = jnp.concatenate([below, block, above], axis=2)
    return wide.reshape(count * rows, 3 * lanes).astype(BF)


def call(kernel, outs, scratch=(), home=False, raw=False, limit=22 << 20):
    single = isinstance(outs, tuple)
    listed = [outs] if single else outs
    home = home if isinstance(home, tuple) else (home,) * len(listed)
    shapes = [
        jax.ShapeDtypeStruct(s, d) if h else pltpu.VMEM(s, d) for (s, d), h in zip(listed, home)
    ]
    vmem = pl.BlockSpec(memory_space=pltpu.VMEM)

    def run(*args):
        if not raw:
            args = [pltpu.with_memory_space_constraint(a, pltpu.VMEM) for a in args]
        got = pl.pallas_call(
            kernel,
            out_shape=shapes,
            in_specs=[vmem] * len(args),
            out_specs=[vmem] * len(shapes),
            scratch_shapes=[pltpu.VMEM(s, d) for s, d in scratch],
            compiler_params=pltpu.CompilerParams(vmem_limit_bytes=limit),
        )(*args)
        return got[0] if single else got

    return run


def dot_rows(dot, rows_ref, weights, put):
    total = rows_ref.shape[0]
    half = (total // 2 + 15) // 16 * 16
    for start, stop in ((0, half), (half, total)):
        got = dot(rows_ref[start:stop], weights)
        put(slice(start // Y, stop // Y), got.reshape((stop - start) // Y, Y, got.shape[1]))


def tap(ref, ox, oy, oz):
    if abs(ox) > 1:
        return jnp.zeros((C, C), BF)
    return ref[9 * (ox + 1) + 3 * (oy + 1) + oz + 1]


def join(a, b):
    return jnp.concatenate([a, b], axis=1)


def forward_weights(up_ref, one_ref, two_ref, w1o_ref, w1x_ref, w2_ref, u_ref):
    zero = jnp.zeros((C, C), BF)
    for oz in (-1, 0, 1):
        for oy in (-1, 0, 1):
            for n, xo in enumerate((0, 1, 2, -1)):
                rows = slice(n * C, n * C + C)
                for p in range(3):
                    ref, at = w1o_ref, (oy + 1) * 128
                    if p:
                        ref, at = w1x_ref, (oy + 1) * 256 + p * 128 - 128
                    pair = [tap(one_ref, XK[2 * p + s] - xo, oy, oz) for s in (0, 1)]
                    ref[oz + 1, rows, at : at + 128] = join(*pair)
            for n, xo in enumerate((0, 1)):
                at_row = (oz + 1) * 128 + n * C
                for p in range(2):
                    at = (oy + 1) * 256 + p * 128
                    pair = [tap(two_ref, XK[2 * p + s] - xo, oy, oz) for s in (0, 1)]
                    w2_ref[at_row : at_row + C, at : at + 128] = join(*pair)
    for e in (0, 1):
        for a in (0, 1):
            for b in (0, 1):
                at = (e * 4 + b * 2 + a) * C
                u_ref[at : at + C, :] = join(up_ref[4 * a + 2 * b + e], zero)
            at = 512 + (e * 2 + a) * C
            lane = iota((C, 128), 1)
            u_ref[at : at + C, :] = ones_where((lane & ~4) == C + 2 * a + e)


def backward_weights(up_ref, one_ref, two_ref, b1o_ref, b1x_ref, b0_ref, ud_ref):
    for oz in (-1, 0, 1):
        for oy in (-1, 0, 1):
            for kk, xk in enumerate(XK):
                ref, at_row = b1x_ref, (oy + 1) * 256 + kk * C - 128
                if kk < 2:
                    ref, at_row = b1o_ref, (oy + 1) * 128 + kk * C
                for p, pair in enumerate(((0, 1), (2, -1))):
                    ref[oz + 1, at_row : at_row + C, p * 128 : p * 128 + 128] = join(
                        *[tap(two_ref, xo - xk, -oy, -oz) for xo in pair]
                    )
            for kk, xk in enumerate(XK[:4]):
                at_row = (oy + 1) * 256 + kk * C
                at = (oz + 1) * 128
                b0_ref[at_row : at_row + C, at : at + 128] = join(
                    *[tap(one_ref, xo - xk, -oy, -oz) for xo in (0, 1)]
                )
    for e in (0, 1):
        for a in (0, 1):
            ud_ref[e, a * C : a * C + C, :] = join(up_ref[4 * a + e], up_ref[4 * a + 2 + e])


def send_kernel(feat_ref, cell_ref, count_ref, out_ref, rows_ref):
    counts = jnp.broadcast_to(count_ref[...].astype(F32), (DEV, DEV)).T
    lane = iota((8, 128), 1)
    for chunk in range(16):
        at = slice(chunk * 128, chunk * 128 + 128)
        feats = feat_ref[0, :, at].astype(F32)
        turned = jnp.concatenate([feats, feats], axis=0).T.reshape(8, 2, 8, 128)
        slots = jnp.where(low_lanes((8, 8, 128)), turned[:, 0], turned[:, 1])
        cells = jnp.broadcast_to(cell_ref[0:1, at].astype(F32), (8, 128))
        cells = pltpu.roll(cells, 0, 1, stride=16, stride_axis=0)
        cells = jnp.concatenate([cells[-d % 8 : -d % 8 + 1] for d in range(8)], axis=0)
        live = lane.astype(F32) < counts[chunk * 8 : chunk * 8 + 8]
        cells = jnp.where(live, cells, NO_CELL)
        for d in range(8):
            row = (chunk * 8 + d) * ROWS
            rows_ref[row : row + 8, :] = slots[d]
            rows_ref[row + 8 : row + 9, :] = cells[d : d + 1]
            rows_ref[row + 9 : row + 10, :] = cells[d : d + 1]
    out_ref[...] = rows_ref[...].astype(BF)


def equal(a, b):
    return jnp.where(a == b, jnp.ones((), BF), jnp.zeros((), BF))


def onehots(recv_ref, rows, wide_ref):
    count = DEV * rows
    lane = iota((1, count), 1)
    sender = lane // rows
    r = lane - sender * rows
    wide_ref[...] = recv_ref[...].astype(F32)
    cells = wide_ref[pl.ds(8, DEV, stride=ROWS), :].astype(BF)
    down = iota((DEV, count), 0)
    here = down == sender
    down = down.astype(F32).astype(BF)
    ids = iota((256, count), 0).astype(F32).astype(BF)
    hot = []
    for h in (0, 1):
        spot = jnp.where(r < 8, r + h * 8, 255).astype(F32).astype(BF)
        values = nn(cells, equal(down, spot))
        cell = jnp.sum(jnp.where(here, values, 0.0), axis=0, keepdims=True)
        cell = jnp.where(r < 8, cell, NO_CELL)
        hot.append(equal(ids, cell.astype(BF)))
    return hot


def grid_kernel(recv_ref, mask_ref, cot_ref, rec_ref, up_ref, down_ref, wide):
    first, second = [nn(hot, recv_ref[...]) for hot in onehots(recv_ref, ROWS, wide)]
    grid = jnp.where(low_lanes(first.shape), first + pltpu.roll(second, C, 1), 0.0).astype(BF)
    row, col = iota((256, 256), 0), iota((256, 256), 1)
    rec = nn(ones_where(col == (row & 3) * K + (row >> 2)), grid)
    kk, zz = iota((K, Y, Z), 0), iota((K, Y, Z), 2)
    zrow, lane = iota((Z, 128), 0), iota((Z, 128), 1)
    marks = jnp.zeros((512, 128), F32)
    for a in (0, 1):
        mine = jnp.where((zz >> 1) == kk, mask_ref[a].astype(F32)[None], 0.0)
        place = ones_where(lane == C + 2 * a + (zrow & 1))
        marks = marks + nn(mine.reshape(512, Z).astype(BF), place)
    odd_y = (iota((512, 128), 0) & 1) == 1
    marks = jnp.where(odd_y, pltpu.roll(marks, 4, 1), marks).astype(BF)
    fold = ones_where((iota((256, 512), 1) >> 1) == iota((256, 512), 0))
    rec = (rec + nn(fold, marks)).reshape(K // 2, Y, 128).astype(BF)
    rec_ref[...] = rec
    up_ref[0:1] = rec_ref[K // 2 - 1 : K // 2]
    up_ref[1:3] = cot_ref[Z - 2 : Z]
    down_ref[0:1] = rec_ref[0:1]
    down_ref[1:3] = cot_ref[0:2]


def side_groups(side, far_pair, near_pair):
    low = jnp.broadcast_to(side[None], near_pair.shape)
    return jnp.where(low, near_pair, far_pair), jnp.where(low, far_pair, near_pair)


def rows_of(rec_ref):
    tiles = rec_ref.shape[0]
    return rec_ref[...].astype(F32).reshape(tiles * Y, 128).astype(BF)


def lift_tile(rec_ref, spread_ref, u_ref, lift, seen):
    kz = 2 * rec_ref.shape[0]
    rec = nn(spread_ref[...], rows_of(rec_ref))
    row, lane = iota(rec.shape, 0), iota(rec.shape, 1)
    rec = jnp.where((lane < C) | ((lane - C) >> 2 == (row & 1)), rec, 0.0).astype(BF)
    odd_row = (iota((kz, Y, 128), 1) & 1) == 1
    for e in (0, 1):
        both = nt(rec, u_ref[e * 256 : e * 256 + 256, :]).reshape(kz, Y, 256)
        live = nt(rec, u_ref[512 + e * 128 : 640 + e * 128, :]).reshape(kz, Y, 128)
        lift[:, e] = live * jnp.where(odd_row, both[:, :, 128:], both[:, :, :128])
        seen[:, e] = live


def own_kernel(
    rec_ref, up_ref, one_ref, two_ref,
    lift, seen, part, u_ref, w1x_ref, w2_ref, spread_ref, w1o_ref, col,
):
    spread_ref[...] = ones_where((iota((544, 272), 0) >> 1) == iota((544, 272), 1))
    forward_weights(up_ref, one_ref, two_ref, w1o_ref, w1x_ref, w2_ref, u_ref)
    lift_tile(rec_ref, spread_ref, u_ref, lift, seen)

    def columns(k0, n):
        own = lift[pl.ds(k0, n)].reshape(2 * n, Y, 128)
        col[pl.ds(pl.multiple_of(k0 * 16, 16), 16 * n), :] = stack_y(own)

    over(KZ, columns, 4)
    for s in range(3):

        def keep(at, value, s=s):
            part[s, at] = value

        dot_rows(nt, col, w1o_ref[s], keep)


def forward_kernel(
    far_ref, near_ref, side_ref, cot_ref,
    lift_own, seen_own, part_own, u_ref, w1x_ref, w2_ref, spread_ref,
    act_ref, delta_ref, dec_ref, slope_ref, lifted_ref, keep_ref,
    lift, seen, mask, col1, part1, col2, part2,
):
    side = side_ref[...] != 0
    for t, ref in enumerate((far_ref, near_ref)):
        lift_tile(ref, spread_ref, u_ref, lift.at[t], seen.at[t])

    def columns(k0, n):
        def load(own_ref, ref):
            three = [own_ref[pl.ds(k0, n)], ref[0, pl.ds(k0, n)], ref[1, pl.ds(k0, n)]]
            three = [v.reshape(2 * n, Y, 128) for v in three]
            return three[0], *side_groups(side, *three[1:])

        own, near, far = load(lift_own, lift)
        at = pl.ds(2 * k0, 2 * n)
        lifted_ref[at] = jnp.concatenate([own, near], axis=2).astype(BF)
        rows = pl.ds(pl.multiple_of(k0 * 16, 16), 16 * n)
        col1[rows, :] = stack_y(jnp.concatenate([near, far], axis=2))
        live_own, live_near, _ = load(seen_own, seen)
        mask[at] = jnp.concatenate([live_own, live_near], axis=2)

    over(KZ, columns, 4)
    for s in range(3):

        def keep1(at, value, s=s):
            part1[s, at] = part_own[s, at] + value

        dot_rows(nt, col1, w1x_ref[s], keep1)

    def first(m, n):
        pre = part1[0, pl.ds(m, n)] + part1[1, pl.ds(m + 1, n)] + part1[2, pl.ds(m + 2, n)]
        live = mask[pl.ds(m + 1, n)]
        sig = jax.nn.sigmoid(pre)
        act = live * (pre * sig)
        slope_ref[pl.ds(m, n)] = live * (sig * (1.0 + pre * (1.0 - sig)))
        act_ref[pl.ds(m, n)] = act.astype(BF)
        col2[pl.ds(pl.multiple_of(m * Y, 16), n * Y), :] = stack_y(act)

    over(2 * KZ - 2, first)

    def keep2(at, value):
        part2[at] = value

    dot_rows(nt, col2, w2_ref[...], keep2)

    def second(q, n):
        pre = (
            part2[pl.ds(q, n), :, 0:128]
            + part2[pl.ds(q + 1, n), :, 128:256]
            + part2[pl.ds(q + 2, n), :, 256:384]
        )
        live = mask[pl.ds(q + 2, n), :, 0:128]
        sig = jax.nn.sigmoid(pre)
        at = pl.ds(q, n)
        dec_ref[at] = (live * (pre * sig)).astype(BF)
        slope = live * (sig * (1.0 + pre * (1.0 - sig)))
        delta_ref[at] = (cot_ref[at].astype(F32) * slope).astype(BF)
        keep_ref[at] = live.astype(BF)

    over(2 * KZ - 4, second)


def wgrad(count, padded, shifted, col, total):
    flat = padded[...].reshape((count + 2) * Y, 128).astype(BF).T
    width = count * Y
    for i, s in enumerate((2, 1, 0)):
        shifted[i * 128 : i * 128 + 128, :] = flat[:, s * Y : s * Y + width]
    for start in (0, 192):
        total[start : start + 192, :] = nn(shifted[start : start + 192, :], col[...])


def packed(block):
    return jnp.concatenate([block[0:32], block[32:64]], axis=1).astype(BF)


def tap_grads(total, put):
    place = {0: 0, 1: 1, 2: 2, -1: 3}
    for ox in (-1, 0, 1):
        for oy in (-1, 0, 1):
            for oz in (-1, 0, 1):
                sums = []
                for x in (0, 1):
                    r = (oz + 1) * 128 + x * C
                    c = (oy + 1) * 256 + place[x + ox] * C
                    sums.append(total[r : r + C, c : c + C])
                put(9 * (ox + 1) + 3 * (oy + 1) + oz + 1, packed(sums[0] + sums[1]))


def second_grad_kernel(
    act_ref, delta_ref, recv_ref, lifted_ref, dec_ref, rec_ref, up_ref, one_ref, two_ref,
    out_ref, hot_ref, part_ref, lifted_col, dec_out, b1x_ref, b0_ref, ud_ref, pick_ref, parent_ref,
    b1o_ref, padded, shifted, col, total, col3, wide,
):
    for h, hot in enumerate(onehots(recv_ref, 8, wide)):
        hot_ref[:, h * 256 : h * 256 + 256] = hot.T
    cell, src = iota((256, 512), 0), iota((256, 512), 1)
    pick_ref[...] = ones_where(src == (cell & (K - 1)) * Y + 2 * (cell >> 6))
    row, lane = iota((K * Y, 128), 0), iota((K * Y, 128), 1)
    rec = nn(ones_where((iota((512, 256), 0) >> 1) == iota((512, 256), 1)), rows_of(rec_ref))
    rec = jnp.where(lane < C, rec, pltpu.roll(rec, C, 1))
    parent_ref[...] = jnp.where(((row & 1) == 0) == (lane < C), rec, 0.0).astype(BF)
    dec_out[...] = dec_ref[2 : 2 + Z]
    backward_weights(up_ref, one_ref, two_ref, b1o_ref, b1x_ref, b0_ref, ud_ref)

    def columns(q, n):
        rows = pl.ds(pl.multiple_of(q * Y, 16), n * Y)
        col3[rows, :] = stack_y(delta_ref[pl.ds(q, n)].astype(F32))
        lifted_col[rows, :] = stack_y(lifted_ref[pl.ds(q + 2, n)].astype(F32))

    over(132, columns)
    for s in range(3):

        def keep(at, value, s=s):
            part_ref[s, at] = value

        dot_rows(nn, col3, b1o_ref[s], keep)
    padded[0:4] = jnp.zeros((4, Y, 128), F32)
    padded[132:136] = jnp.zeros((4, Y, 128), F32)
    padded[4:132] = delta_ref[2:130].astype(F32)
    def act_col(m, n):
        rows = pl.ds(pl.multiple_of(m * Y, 16), n * Y)
        col[rows, :] = stack_y(act_ref[pl.ds(m, n)].astype(F32))

    over(134, act_col)
    wgrad(134, padded, shifted, col, total)

    def put(t, block):
        out_ref[t] = block

    tap_grads(total, put)


def backward_kernel(
    far_ref, near_ref, side_ref, slope_ref, keep_ref, hot_ref, part_own, lifted_col, two_ref,
    b1x_ref, b0_ref, ud_ref, pick_ref, parent_ref, out_ref,
    col3, part3, col4, part4, padded, shifted, total, du,
):
    side = side_ref[...] != 0

    def columns(q, n):
        at = pl.ds(q, n)
        groups = side_groups(side, far_ref[at].astype(F32), near_ref[at].astype(F32))
        rows = pl.ds(pl.multiple_of(q * Y, 16), n * Y)
        col3[rows, :] = stack_y(jnp.concatenate(groups, axis=2))

    over(132, columns)
    for s in range(3):

        def keep3(at, value, s=s):
            part3[s, at] = part_own[s, at] + value

        dot_rows(nn, col3, b1x_ref[s], keep3)

    def first(r, n):
        back = part3[0, pl.ds(r, n)] + part3[1, pl.ds(r + 1, n)] + part3[2, pl.ds(r + 2, n)]
        delta = back * slope_ref[pl.ds(r + 2, n)]
        padded[pl.ds(r + 2, n)] = delta[:, :, 0:128]
        col4[pl.ds(pl.multiple_of(r * Y, 16), n * Y), :] = stack_y(delta)

    over(130, first)
    padded[0:3] = jnp.zeros((3, Y, 128), F32)
    padded[131:134] = jnp.zeros((3, Y, 128), F32)

    def keep4(at, value):
        part4[at] = value

    dot_rows(nn, col4, b0_ref[...], keep4)

    def upper(z, n):
        back = (
            part4[pl.ds(z, n), :, 0:128]
            + part4[pl.ds(z + 1, n), :, 128:256]
            + part4[pl.ds(z + 2, n), :, 256:384]
        )
        value = keep_ref[pl.ds(z + 2, n)].astype(F32) * back
        du[pl.ds(z >> 1, n // 2)] = value.reshape(n // 2, 2, Y, 128)

    over(Z, upper)

    split = [du[:, e].reshape(K * Y, 128).astype(BF) for e in (0, 1)]
    row, lane = iota((K * Y, 128), 0), iota((K * Y, 128), 1)
    match = ((row & 1) == 0) == (lane < C)
    summed = nn(split[0], ud_ref[0]) + nn(split[1], ud_ref[1])
    summed = jnp.where(match, summed, 0.0).reshape(K, Y, 128)
    summed = summed + pltpu.roll(summed, Y - 1, 1)
    summed = summed + pltpu.roll(summed, C, 2)
    parent = summed.reshape(K * Y, 128).astype(BF)
    parent = nn(pick_ref[...], parent)
    low = low_lanes(parent.shape)
    sides = [jnp.where(low, parent, 0.0), jnp.where(low, 0.0, parent)]
    slots = nn(hot_ref[...], jnp.concatenate(sides, axis=0).astype(BF))
    out_ref[:, 0:8, :] = slots.reshape(DEV, 8, 128).astype(BF)

    def put(index, block):
        out_ref[2 * index, 8:24, :] = block[0:16]
        out_ref[2 * index + 1, 8:24, :] = block[16:32]

    for e in (0, 1):
        up_grad = tn(split[e], parent_ref[...])
        for a in (0, 1):
            for b in (0, 1):
                block = up_grad[a * C : a * C + C, b * C : b * C + C]
                put(54 + 4 * a + 2 * b + e, packed(block))
    wgrad(132, padded, shifted, lifted_col, total)
    tap_grads(total, lambda t, block: put(27 + t, block))
    for t in range(27):
        put(t, two_ref[t])
    out_ref[124:128, 8:24, :] = jnp.zeros((4, 16, 128), BF)


def sum_kernel(recv_ref, out_ref, *, scale):
    def one(i, total):
        return total + jnp.sum(recv_ref[pl.ds(i * 8, 8), 8:24, :].astype(F32), axis=0)

    total = lax.fori_loop(0, 16, one, jnp.zeros((16, 128), F32))
    out_ref[...] = jnp.broadcast_to((total * scale).astype(BF)[None], out_ref.shape)


def slot_kernel(recv_ref, out_ref):
    for chunk in range(16):
        block = recv_ref[chunk * 8 : chunk * 8 + 8, 0:8, :].astype(F32)
        halves = [block[:, None], pltpu.roll(block, C, 2)[:, None]]
        turned = jnp.concatenate(halves, axis=1).reshape(128, 128).T
        out_ref[0, :, chunk * 128 : chunk * 128 + 128] = turned[0:C].astype(BF)


def unpack_kernel(recv_ref, one_ref, two_ref, up_ref):
    def matrix(index):
        top = recv_ref[2 * index].astype(F32)
        low = recv_ref[2 * index + 1].astype(F32)
        both = jnp.concatenate([top, low], axis=0)
        return jnp.concatenate([both[:, :C], both[:, C:]], axis=0)

    for t in range(27):
        two_ref[t] = matrix(t)
        one_ref[t] = matrix(27 + t)
    for o in range(8):
        up_ref[o] = matrix(54 + o)


def swap(array, axis, first):
    count = lax.axis_size(axis)
    pairs = [(i, i + 1) for i in range(first, count - 1, 2)]
    return lax.ppermute(array, axis, pairs + [(j, i) for i, j in pairs])


def swaps(far, near, axis):
    return swap(far, axis, 1), swap(near, axis, 0)


def exchange(array):
    return lax.all_to_all(array, ("gz", "xy"), 0, 0, tiled=True)


def local(
    parent_feat, parent_cell, send_count, up_weight, conv_one, conv_two, child_mask, cotangent
):
    size_x, size_y, size_z = cotangent.shape[1:]
    voxels = size_x * size_y * size_z * lax.axis_size("xy") * lax.axis_size("gz")
    scale = 1.0 / math.sqrt(voxels)
    sent = call(send_kernel, ((DEV * ROWS, 128), BF), [((DEV * ROWS, 128), F32)], raw=True, limit=58 << 20)(
        parent_feat, parent_cell, send_count
    )
    recv = exchange(sent.reshape(DEV, ROWS // 2, 2, 128)).reshape(DEV * ROWS, 128)
    cot = cotangent.transpose(3, 2, 1, 0).reshape(Z, Y, 128)
    rec, up_edge, down_edge = call(
        grid_kernel,
        [((K // 2, Y, 128), BF), ((3, Y, 128), BF), ((3, Y, 128), BF)],
        [((DEV * ROWS, 128), F32)],
    )(recv, child_mask, cot)
    odd_z = lax.axis_index("gz") % 2 == 1
    far, near = swaps(
        jnp.where(odd_z, up_edge, down_edge), jnp.where(odd_z, down_edge, up_edge), "gz"
    )
    before, after = jnp.where(odd_z, near, far), jnp.where(odd_z, far, near)
    rec_ext = jnp.concatenate([before[0:1], rec, after[0:1]], axis=0)
    cot_ext = jnp.concatenate([before[1:3], cot, after[1:3]], axis=0)
    even_x = lax.axis_index("xy") % 2 == 0
    side = (low_lanes((8, 128)) == even_x).astype(jnp.int32)
    rec_far, rec_near = swaps(rec_ext, rec_ext, "xy")
    weights = up_weight, conv_one, conv_two
    lift_own, seen_own, part_own, u, w1x, w2, spread = call(
        own_kernel,
        [
            ((KZ, 2, Y, 128), F32), ((KZ, 2, Y, 128), F32), ((3, 136, Y, 256), F32),
            ((768, 128), BF), ((3, 256, 768), BF), ((384, 768), BF), ((544, 272), BF),
        ],
        [((3, 256, 384), BF), ((1088, 384), BF)],
    )(rec_ext, *weights)
    act, delta, dec, slope, lifted, keep = call(
        forward_kernel,
        [
            ((134, Y, 256), BF), ((132, Y, 128), BF), ((132, Y, 128), BF),
            ((134, Y, 256), F32), ((136, Y, 256), BF), ((132, Y, 128), BF),
        ],
        [
            ((2, KZ, 2, Y, 128), F32), ((2, KZ, 2, Y, 128), F32), ((136, Y, 256), F32),
            ((1088, 768), BF), ((3, 136, Y, 256), F32), ((1072, 768), BF), ((134, Y, 384), F32),
        ],
    )(rec_far, rec_near, side, cot_ext, lift_own, seen_own, part_own, u, w1x, w2, spread)
    delta_far, delta_near = swaps(delta, delta, "xy")
    two, hot, part_back, lifted_col, dec, b1x, b0, ud, pick, parent = call(
        second_grad_kernel,
        [
            ((27, 32, 128), BF), ((1024, 512), BF), ((3, 132, Y, 256), F32), ((1056, 768), BF),
            ((Z, Y, 128), BF), ((3, 768, 256), BF), ((768, 384), BF), ((2, 128, 128), BF),
            ((256, 512), BF), ((512, 128), BF),
        ],
        [
            ((3, 384, 256), BF), ((136, Y, 128), F32), ((384, 1072), BF), ((1072, 768), BF), ((384, 768), F32),
            ((1056, 384), BF), ((DEV * ROWS, 128), F32),
        ],
        home=(False, False, False, False, True, *[False] * 5),
    )(act, delta, recv, lifted, dec, rec, *weights)
    decoded = dec.reshape(Z, Y, 2, C).transpose(3, 2, 1, 0)
    message = call(
        backward_kernel,
        ((DEV, 24, 128), BF),
        [
            ((1056, 768), BF), ((3, 132, Y, 256), F32), ((1040, 768), BF), ((130, Y, 384), F32),
            ((134, Y, 128), F32), ((384, 1056), BF), ((384, 768), F32), ((K, 2, Y, 128), F32),
        ],
    )(
        delta_far, delta_near, side, slope, keep, hot, part_back, lifted_col, two, b1x, b0, ud, pick, parent
    )
    back = exchange(message)
    total = call(functools.partial(sum_kernel, scale=scale), ((DEV, 16, 128), BF))(back)
    gathered = exchange(total)
    grad_parent = call(slot_kernel, ((1, C, 2048), BF), home=True)(back)
    grad_one, grad_two, grad_up = call(
        unpack_kernel, [((27, C, C), F32), ((27, C, C), F32), ((8, C, C), F32)], home=True
    )(gathered)
    return decoded, grad_parent, grad_one, grad_two, grad_up


def solution(mesh):
    placed = (
        P(("gz", "xy"), None, None),
        P(("gz", "xy"), None),
        P(("gz", "xy"), None),
        P(),
        P(),
        P(),
        P("xy", None, "gz"),
        P(None, "xy", None, "gz"),
    )
    return jax.shard_map(
        local,
        mesh=mesh,
        in_specs=placed,
        out_specs=(P(None, "xy", None, "gz"), P(("gz", "xy"), None, None), P(), P(), P()),
        check_vma=False,
    )
```

```python
import functools
import math

import jax
import jax.numpy as jnp
from jax import lax
from jax.experimental import pallas as pl
from jax.experimental.pallas import tpu as pltpu
from jax.sharding import PartitionSpec as P

BF = jnp.bfloat16
F32 = jnp.float32
XK = (0, 1, 2, -1, -2, 3)
C = 64
Z = 128
Y = 8
K = 64
KZ = K + 4
DEV = 128
NO_CELL = 256.0
ROWS = 10
STEP = 8


def iota(shape, dim):
    return lax.broadcasted_iota(jnp.int32, shape, dim)


def ones_where(cond):
    return jnp.where(cond, 1.0, 0.0).astype(BF)


def nt(a, b):
    return lax.dot_general(a, b, (((1,), (1,)), ((), ())), preferred_element_type=F32)


def nn(a, b):
    return lax.dot_general(a, b, (((1,), (0,)), ((), ())), preferred_element_type=F32)


def tn(a, b):
    return lax.dot_general(a, b, (((0,), (0,)), ((), ())), preferred_element_type=F32)


def over(total, body, step=STEP):
    full = total // step

    def one(i, carry):
        body(pl.multiple_of(i * step, step), step)
        return carry

    lax.fori_loop(0, full, one, 0)
    if total % step:
        body(full * step, total % step)


def low_lanes(shape):
    return iota(shape, len(shape) - 1) < C


def stack_y(block):
    count, rows, lanes = block.shape
    row = iota(block.shape, 1)
    below = jnp.where(row == 0, 0.0, pltpu.roll(block, 1, 1))
    above = jnp.where(row == rows - 1, 0.0, pltpu.roll(block, rows - 1, 1))
    wide = jnp.concatenate([below, block, above], axis=2)
    return wide.reshape(count * rows, 3 * lanes).astype(BF)


def call(kernel, outs, scratch=(), home=False, raw=False, limit=22 << 20):
    single = isinstance(outs, tuple)
    listed = [outs] if single else outs
    home = home if isinstance(home, tuple) else (home,) * len(listed)
    shapes = [
        jax.ShapeDtypeStruct(s, d) if h else pltpu.VMEM(s, d) for (s, d), h in zip(listed, home)
    ]
    vmem = pl.BlockSpec(memory_space=pltpu.VMEM)

    def run(*args):
        if not raw:
            args = [pltpu.with_memory_space_constraint(a, pltpu.VMEM) for a in args]
        got = pl.pallas_call(
            kernel,
            out_shape=shapes,
            in_specs=[vmem] * len(args),
            out_specs=[vmem] * len(shapes),
            scratch_shapes=[pltpu.VMEM(s, d) for s, d in scratch],
            compiler_params=pltpu.CompilerParams(vmem_limit_bytes=limit),
        )(*args)
        return got[0] if single else got

    return run


def dot_rows(dot, rows_ref, weights, put):
    total = rows_ref.shape[0]
    half = (total // 2 + 15) // 16 * 16
    for start, stop in ((0, half), (half, total)):
        got = dot(rows_ref[start:stop], weights)
        put(slice(start // Y, stop // Y), got.reshape((stop - start) // Y, Y, got.shape[1]))


def tap(ref, ox, oy, oz):
    if abs(ox) > 1:
        return jnp.zeros((C, C), BF)
    return ref[9 * (ox + 1) + 3 * (oy + 1) + oz + 1]


def join(a, b):
    return jnp.concatenate([a, b], axis=1)


def first_weights(one_ref, own_ref, outer_ref):
    for oz in (-1, 0, 1):
        for oy in (-1, 0, 1):
            for n, xo in enumerate((0, 1, 2, -1)):
                rows = slice(n * C, n * C + C)
                for p in range(3):
                    ref, at = own_ref, (oy + 1) * 128
                    if p:
                        ref, at = outer_ref, (oy + 1) * 256 + p * 128 - 128
                    if ref is None:
                        continue
                    pair = [tap(one_ref, XK[2 * p + s] - xo, oy, oz) for s in (0, 1)]
                    ref[oz + 1, rows, at : at + 128] = join(*pair)


def second_weights(two_ref, w2_ref):
    for oz in (-1, 0, 1):
        for oy in (-1, 0, 1):
            for n, xo in enumerate((0, 1)):
                at_row = (oz + 1) * 128 + n * C
                for p in range(2):
                    at = (oy + 1) * 256 + p * 128
                    pair = [tap(two_ref, XK[2 * p + s] - xo, oy, oz) for s in (0, 1)]
                    w2_ref[at_row : at_row + C, at : at + 128] = join(*pair)


def lift_weights(up_ref, u_ref):
    zero = jnp.zeros((C, C), BF)
    for e in (0, 1):
        for a in (0, 1):
            for b in (0, 1):
                at = (e * 4 + b * 2 + a) * C
                u_ref[at : at + C, :] = join(up_ref[4 * a + 2 * b + e], zero)
            at = 512 + (e * 2 + a) * C
            lane = iota((C, 128), 1)
            u_ref[at : at + C, :] = ones_where((lane & ~4) == C + 2 * a + e)


def backward_weights(up_ref, one_ref, two_ref, b1o_ref, b1x_ref, b0_ref, ud_ref):
    for oz in (-1, 0, 1):
        for oy in (-1, 0, 1):
            for kk, xk in enumerate(XK):
                ref, at_row = b1x_ref, (oy + 1) * 256 + kk * C - 128
                if kk < 2:
                    ref, at_row = b1o_ref, (oy + 1) * 128 + kk * C
                for p, pair in enumerate(((0, 1), (2, -1))):
                    ref[oz + 1, at_row : at_row + C, p * 128 : p * 128 + 128] = join(
                        *[tap(two_ref, xo - xk, -oy, -oz) for xo in pair]
                    )
            for kk, xk in enumerate(XK[:4]):
                at_row = (oy + 1) * 256 + kk * C
                at = (oz + 1) * 128
                b0_ref[at_row : at_row + C, at : at + 128] = join(
                    *[tap(one_ref, xo - xk, -oy, -oz) for xo in (0, 1)]
                )
    for e in (0, 1):
        for a in (0, 1):
            ud_ref[e, a * C : a * C + C, :] = join(up_ref[4 * a + e], up_ref[4 * a + 2 + e])


def send_kernel(feat_ref, cell_ref, count_ref, out_ref, rows_ref):
    counts = jnp.broadcast_to(count_ref[...].astype(F32), (DEV, DEV)).T
    lane = iota((8, 128), 1)
    for chunk in range(16):
        at = slice(chunk * 128, chunk * 128 + 128)
        feats = feat_ref[0, :, at].astype(F32)
        turned = jnp.concatenate([feats, feats], axis=0).T.reshape(8, 2, 8, 128)
        slots = jnp.where(low_lanes((8, 8, 128)), turned[:, 0], turned[:, 1])
        cells = jnp.broadcast_to(cell_ref[0:1, at].astype(F32), (8, 128))
        cells = pltpu.roll(cells, 0, 1, stride=16, stride_axis=0)
        cells = jnp.concatenate([cells[-d % 8 : -d % 8 + 1] for d in range(8)], axis=0)
        live = lane.astype(F32) < counts[chunk * 8 : chunk * 8 + 8]
        cells = jnp.where(live, cells, NO_CELL)
        for d in range(8):
            row = (chunk * 8 + d) * ROWS
            rows_ref[row : row + 8, :] = slots[d]
            rows_ref[row + 8 : row + 9, :] = cells[d : d + 1]
            rows_ref[row + 9 : row + 10, :] = cells[d : d + 1]
    out_ref[...] = rows_ref[...].astype(BF)


def equal(a, b):
    return jnp.where(a == b, jnp.ones((), BF), jnp.zeros((), BF))


def onehots(recv_ref, rows, wide_ref):
    count = DEV * rows
    lane = iota((1, count), 1)
    sender = lane // rows
    r = lane - sender * rows
    wide_ref[...] = recv_ref[...].astype(F32)
    cells = wide_ref[pl.ds(8, DEV, stride=ROWS), :].astype(BF)
    down = iota((DEV, count), 0)
    here = down == sender
    down = down.astype(F32).astype(BF)
    ids = iota((256, count), 0).astype(F32).astype(BF)
    hot = []
    for h in (0, 1):
        spot = jnp.where(r < 8, r + h * 8, 255).astype(F32).astype(BF)
        values = nn(cells, equal(down, spot))
        cell = jnp.sum(jnp.where(here, values, 0.0), axis=0, keepdims=True)
        cell = jnp.where(r < 8, cell, NO_CELL)
        hot.append(equal(ids, cell.astype(BF)))
    return hot


def prepare_kernel(
    mask_ref, up_ref, one_ref, marks_ref, spread_ref, w1x_ref, u_ref
):
    kk, zz = iota((K, Y, Z), 0), iota((K, Y, Z), 2)
    zrow, lane = iota((Z, 128), 0), iota((Z, 128), 1)
    marks = jnp.zeros((512, 128), F32)
    for a in (0, 1):
        mine = jnp.where((zz >> 1) == kk, mask_ref[a].astype(F32)[None], 0.0)
        place = ones_where(lane == C + 2 * a + (zrow & 1))
        marks = marks + nn(mine.reshape(512, Z).astype(BF), place)
    odd_y = (iota((512, 128), 0) & 1) == 1
    marks = jnp.where(odd_y, pltpu.roll(marks, 4, 1), marks).astype(BF)
    fold = ones_where((iota((256, 512), 1) >> 1) == iota((256, 512), 0))
    marks_ref[...] = nn(fold, marks)
    spread_ref[...] = ones_where((iota((544, 272), 0) >> 1) == iota((544, 272), 1))
    first_weights(one_ref, None, w1x_ref)
    lift_weights(up_ref, u_ref)


def grid_kernel(recv_ref, marks_ref, cot_ref, rec_ref, up_ref, down_ref, wide):
    first, second = [nn(hot, recv_ref[...]) for hot in onehots(recv_ref, ROWS, wide)]
    grid = jnp.where(low_lanes(first.shape), first + pltpu.roll(second, C, 1), 0.0).astype(BF)
    row, col = iota((256, 256), 0), iota((256, 256), 1)
    pick = ones_where(col == (row & 3) * K + (row >> 2))
    rec = (nn(pick, grid) + marks_ref[...]).reshape(K // 2, Y, 128).astype(BF)
    rec_ref[...] = rec
    up_ref[0:1] = rec_ref[K // 2 - 1 : K // 2]
    up_ref[1:3] = cot_ref[Z - 2 : Z]
    down_ref[0:1] = rec_ref[0:1]
    down_ref[1:3] = cot_ref[0:2]


def side_groups(side, far_pair, near_pair):
    low = jnp.broadcast_to(side[None], near_pair.shape)
    return jnp.where(low, near_pair, far_pair), jnp.where(low, far_pair, near_pair)


def rows_of(rec_ref):
    tiles = rec_ref.shape[0]
    return rec_ref[...].astype(F32).reshape(tiles * Y, 128).astype(BF)


def lift_tile(rec_ref, spread_ref, u_ref, lift, seen):
    kz = 2 * rec_ref.shape[0]
    rec = nn(spread_ref[...], rows_of(rec_ref))
    row, lane = iota(rec.shape, 0), iota(rec.shape, 1)
    rec = jnp.where((lane < C) | ((lane - C) >> 2 == (row & 1)), rec, 0.0).astype(BF)
    odd_row = (iota((kz, Y, 128), 1) & 1) == 1
    for e in (0, 1):
        both = nt(rec, u_ref[e * 256 : e * 256 + 256, :]).reshape(kz, Y, 256)
        live = nt(rec, u_ref[512 + e * 128 : 640 + e * 128, :]).reshape(kz, Y, 128)
        lift[:, e] = live * jnp.where(odd_row, both[:, :, 128:], both[:, :, :128])
        seen[:, e] = live


def own_kernel(
    rec_ref, spread_ref, u_ref, one_ref, two_ref, lift, seen, part, w2_ref, w1o_ref, col
):
    first_weights(one_ref, w1o_ref, None)
    second_weights(two_ref, w2_ref)
    lift_tile(rec_ref, spread_ref, u_ref, lift, seen)

    def columns(k0, n):
        own = lift[pl.ds(k0, n)].reshape(2 * n, Y, 128)
        col[pl.ds(pl.multiple_of(k0 * 16, 16), 16 * n), :] = stack_y(own)

    over(KZ, columns, 4)
    for s in range(3):

        def keep(at, value, s=s):
            part[s, at] = value

        dot_rows(nt, col, w1o_ref[s], keep)


def forward_kernel(
    far_ref, near_ref, side_ref, cot_ref,
    lift_own, seen_own, part_own, u_ref, w1x_ref, w2_ref, spread_ref,
    act_ref, delta_ref, dec_ref, pre_ref, lifted_ref, keep_ref, mask,
    lift, seen, col1, part1, col2, part2,
):
    side = side_ref[...] != 0
    for t, ref in enumerate((far_ref, near_ref)):
        lift_tile(ref, spread_ref, u_ref, lift.at[t], seen.at[t])

    def columns(k0, n):
        def load(own_ref, ref):
            three = [own_ref[pl.ds(k0, n)], ref[0, pl.ds(k0, n)], ref[1, pl.ds(k0, n)]]
            three = [v.reshape(2 * n, Y, 128) for v in three]
            return three[0], *side_groups(side, *three[1:])

        own, near, far = load(lift_own, lift)
        at = pl.ds(2 * k0, 2 * n)
        lifted_ref[at] = jnp.concatenate([own, near], axis=2).astype(BF)
        rows = pl.ds(pl.multiple_of(k0 * 16, 16), 16 * n)
        col1[rows, :] = stack_y(jnp.concatenate([near, far], axis=2))
        live_own, live_near, _ = load(seen_own, seen)
        mask[at] = jnp.concatenate([live_own, live_near], axis=2)

    over(KZ, columns, 4)
    for s in range(3):

        def keep1(at, value, s=s):
            part1[s, at] = part_own[s, at] + value

        dot_rows(nt, col1, w1x_ref[s], keep1)

    def first(m, n):
        pre = part1[0, pl.ds(m, n)] + part1[1, pl.ds(m + 1, n)] + part1[2, pl.ds(m + 2, n)]
        live = mask[pl.ds(m + 1, n)]
        sig = jax.nn.sigmoid(pre)
        act = live * (pre * sig)
        pre_ref[pl.ds(m, n)] = pre
        act_ref[pl.ds(m, n)] = act.astype(BF)
        col2[pl.ds(pl.multiple_of(m * Y, 16), n * Y), :] = stack_y(act)

    over(2 * KZ - 2, first)

    def keep2(at, value):
        part2[at] = value

    dot_rows(nt, col2, w2_ref[...], keep2)

    def second(q, n):
        pre = (
            part2[pl.ds(q, n), :, 0:128]
            + part2[pl.ds(q + 1, n), :, 128:256]
            + part2[pl.ds(q + 2, n), :, 256:384]
        )
        live = mask[pl.ds(q + 2, n), :, 0:128]
        sig = jax.nn.sigmoid(pre)
        at = pl.ds(q, n)
        dec_ref[at] = (live * (pre * sig)).astype(BF)
        slope = live * (sig * (1.0 + pre * (1.0 - sig)))
        delta_ref[at] = (cot_ref[at].astype(F32) * slope).astype(BF)
        keep_ref[at] = live.astype(BF)

    over(2 * KZ - 4, second)


def wgrad(count, padded, shifted, col, total):
    flat = padded[...].reshape((count + 2) * Y, 128).astype(BF).T
    width = count * Y
    for i, s in enumerate((2, 1, 0)):
        shifted[i * 128 : i * 128 + 128, :] = flat[:, s * Y : s * Y + width]
    for start in (0, 192):
        total[start : start + 192, :] = nn(shifted[start : start + 192, :], col[...])


def packed(block):
    return jnp.concatenate([block[0:32], block[32:64]], axis=1).astype(BF)


def tap_grads(total, put):
    place = {0: 0, 1: 1, 2: 2, -1: 3}
    for ox in (-1, 0, 1):
        for oy in (-1, 0, 1):
            for oz in (-1, 0, 1):
                sums = []
                for x in (0, 1):
                    r = (oz + 1) * 128 + x * C
                    c = (oy + 1) * 256 + place[x + ox] * C
                    sums.append(total[r : r + C, c : c + C])
                put(9 * (ox + 1) + 3 * (oy + 1) + oz + 1, packed(sums[0] + sums[1]))


def second_grad_kernel(
    act_ref, delta_ref, recv_ref, lifted_ref, dec_ref, rec_ref, pre_ref, mask_ref,
    up_ref, one_ref, two_ref,
    out_ref, hot_ref, part_ref, lifted_col, dec_out, b1x_ref, b0_ref, ud_ref, pick_ref, parent_ref,
    slope_ref,
    b1o_ref, padded, shifted, col, total, col3, wide,
):
    for h, hot in enumerate(onehots(recv_ref, 8, wide)):
        hot_ref[:, h * 256 : h * 256 + 256] = hot.T
    cell, src = iota((256, 512), 0), iota((256, 512), 1)
    pick_ref[...] = ones_where(src == (cell & (K - 1)) * Y + 2 * (cell >> 6))
    row, lane = iota((K * Y, 128), 0), iota((K * Y, 128), 1)
    rec = nn(ones_where((iota((512, 256), 0) >> 1) == iota((512, 256), 1)), rows_of(rec_ref))
    rec = jnp.where(lane < C, rec, pltpu.roll(rec, C, 1))
    parent_ref[...] = jnp.where(((row & 1) == 0) == (lane < C), rec, 0.0).astype(BF)
    dec_out[...] = dec_ref[2 : 2 + Z]
    backward_weights(up_ref, one_ref, two_ref, b1o_ref, b1x_ref, b0_ref, ud_ref)

    def columns(q, n):
        rows = pl.ds(pl.multiple_of(q * Y, 16), n * Y)
        col3[rows, :] = stack_y(delta_ref[pl.ds(q, n)].astype(F32))
        lifted_col[rows, :] = stack_y(lifted_ref[pl.ds(q + 2, n)].astype(F32))

    over(132, columns)
    for s in range(3):

        def keep(at, value, s=s):
            part_ref[s, at] = value

        dot_rows(nn, col3, b1o_ref[s], keep)
    padded[0:4] = jnp.zeros((4, Y, 128), F32)
    padded[132:136] = jnp.zeros((4, Y, 128), F32)
    padded[4:132] = delta_ref[2:130].astype(F32)
    def act_col(m, n):
        pre = pre_ref[pl.ds(m, n)]
        sig = jax.nn.sigmoid(pre)
        slope_ref[pl.ds(m, n)] = mask_ref[pl.ds(m + 1, n)] * (sig * (1.0 + pre * (1.0 - sig)))
        rows = pl.ds(pl.multiple_of(m * Y, 16), n * Y)
        col[rows, :] = stack_y(act_ref[pl.ds(m, n)].astype(F32))

    over(134, act_col)
    wgrad(134, padded, shifted, col, total)

    def put(t, block):
        out_ref[t] = block

    tap_grads(total, put)


def backward_kernel(
    far_ref, near_ref, side_ref, slope_ref, keep_ref, hot_ref, part_own, lifted_col, two_ref,
    b1x_ref, b0_ref, ud_ref, pick_ref, parent_ref, out_ref,
    col3, part3, col4, part4, padded, shifted, total, du,
):
    side = side_ref[...] != 0

    def columns(q, n):
        at = pl.ds(q, n)
        groups = side_groups(side, far_ref[at].astype(F32), near_ref[at].astype(F32))
        rows = pl.ds(pl.multiple_of(q * Y, 16), n * Y)
        col3[rows, :] = stack_y(jnp.concatenate(groups, axis=2))

    over(132, columns)
    for s in range(3):

        def keep3(at, value, s=s):
            part3[s, at] = part_own[s, at] + value

        dot_rows(nn, col3, b1x_ref[s], keep3)

    def first(r, n):
        back = part3[0, pl.ds(r, n)] + part3[1, pl.ds(r + 1, n)] + part3[2, pl.ds(r + 2, n)]
        delta = back * slope_ref[pl.ds(r + 2, n)]
        padded[pl.ds(r + 2, n)] = delta[:, :, 0:128]
        col4[pl.ds(pl.multiple_of(r * Y, 16), n * Y), :] = stack_y(delta)

    over(130, first)
    padded[0:3] = jnp.zeros((3, Y, 128), F32)
    padded[131:134] = jnp.zeros((3, Y, 128), F32)

    def keep4(at, value):
        part4[at] = value

    dot_rows(nn, col4, b0_ref[...], keep4)

    def upper(z, n):
        back = (
            part4[pl.ds(z, n), :, 0:128]
            + part4[pl.ds(z + 1, n), :, 128:256]
            + part4[pl.ds(z + 2, n), :, 256:384]
        )
        value = keep_ref[pl.ds(z + 2, n)].astype(F32) * back
        du[pl.ds(z >> 1, n // 2)] = value.reshape(n // 2, 2, Y, 128)

    over(Z, upper)

    split = [du[:, e].reshape(K * Y, 128).astype(BF) for e in (0, 1)]
    row, lane = iota((K * Y, 128), 0), iota((K * Y, 128), 1)
    match = ((row & 1) == 0) == (lane < C)
    summed = nn(split[0], ud_ref[0]) + nn(split[1], ud_ref[1])
    summed = jnp.where(match, summed, 0.0).reshape(K, Y, 128)
    summed = summed + pltpu.roll(summed, Y - 1, 1)
    summed = summed + pltpu.roll(summed, C, 2)
    parent = summed.reshape(K * Y, 128).astype(BF)
    parent = nn(pick_ref[...], parent)
    low = low_lanes(parent.shape)
    sides = [jnp.where(low, parent, 0.0), jnp.where(low, 0.0, parent)]
    slots = nn(hot_ref[...], jnp.concatenate(sides, axis=0).astype(BF))
    out_ref[:, 0:8, :] = slots.reshape(DEV, 8, 128).astype(BF)

    def put(index, block):
        out_ref[2 * index, 8:24, :] = block[0:16]
        out_ref[2 * index + 1, 8:24, :] = block[16:32]

    for e in (0, 1):
        up_grad = tn(split[e], parent_ref[...])
        for a in (0, 1):
            for b in (0, 1):
                block = up_grad[a * C : a * C + C, b * C : b * C + C]
                put(54 + 4 * a + 2 * b + e, packed(block))
    wgrad(132, padded, shifted, lifted_col, total)
    tap_grads(total, lambda t, block: put(27 + t, block))
    for t in range(27):
        put(t, two_ref[t])
    out_ref[124:128, 8:24, :] = jnp.zeros((4, 16, 128), BF)


def sum_kernel(recv_ref, out_ref, *, scale):
    def one(i, total):
        return total + jnp.sum(recv_ref[pl.ds(i * 8, 8), 8:24, :].astype(F32), axis=0)

    total = lax.fori_loop(0, 16, one, jnp.zeros((16, 128), F32))
    out_ref[...] = jnp.broadcast_to((total * scale).astype(BF)[None], out_ref.shape)


def slot_kernel(recv_ref, out_ref):
    for chunk in range(16):
        block = recv_ref[chunk * 8 : chunk * 8 + 8, 0:8, :].astype(F32)
        halves = [block[:, None], pltpu.roll(block, C, 2)[:, None]]
        turned = jnp.concatenate(halves, axis=1).reshape(128, 128).T
        out_ref[0, :, chunk * 128 : chunk * 128 + 128] = turned[0:C].astype(BF)


def unpack_kernel(recv_ref, one_ref, two_ref, up_ref):
    def matrix(index):
        top = recv_ref[2 * index].astype(F32)
        low = recv_ref[2 * index + 1].astype(F32)
        both = jnp.concatenate([top, low], axis=0)
        return jnp.concatenate([both[:, :C], both[:, C:]], axis=0)

    for t in range(27):
        two_ref[t] = matrix(t)
        one_ref[t] = matrix(27 + t)
    for o in range(8):
        up_ref[o] = matrix(54 + o)


def swap(array, axis, first):
    count = lax.axis_size(axis)
    pairs = [(i, i + 1) for i in range(first, count - 1, 2)]
    return lax.ppermute(array, axis, pairs + [(j, i) for i, j in pairs])


def swaps(far, near, axis):
    return swap(far, axis, 1), swap(near, axis, 0)


def exchange(array):
    return lax.all_to_all(array, ("gz", "xy"), 0, 0, tiled=True)


def local(
    parent_feat, parent_cell, send_count, up_weight, conv_one, conv_two, child_mask, cotangent
):
    size_x, size_y, size_z = cotangent.shape[1:]
    voxels = size_x * size_y * size_z * lax.axis_size("xy") * lax.axis_size("gz")
    scale = 1.0 / math.sqrt(voxels)
    sent = call(send_kernel, ((DEV * ROWS, 128), BF), [((DEV * ROWS, 128), F32)], raw=True, limit=58 << 20)(
        parent_feat, parent_cell, send_count
    )
    sent, child_mask = lax.optimization_barrier((sent, child_mask))
    recv = exchange(sent.reshape(DEV, ROWS // 2, 2, 128)).reshape(DEV * ROWS, 128)
    cot = cotangent.transpose(3, 2, 1, 0).reshape(Z, Y, 128)
    weights = up_weight, conv_one, conv_two
    marks, spread, w1x, u = call(
        prepare_kernel,
        [
            ((256, 128), F32), ((544, 272), BF), ((3, 256, 768), BF), ((768, 128), BF),
        ],
    )(child_mask, up_weight, conv_one)
    rec, up_edge, down_edge = call(
        grid_kernel,
        [((K // 2, Y, 128), BF), ((3, Y, 128), BF), ((3, Y, 128), BF)],
        [((DEV * ROWS, 128), F32)],
    )(recv, marks, cot)
    odd_z = lax.axis_index("gz") % 2 == 1
    far, near = swaps(
        jnp.where(odd_z, up_edge, down_edge), jnp.where(odd_z, down_edge, up_edge), "gz"
    )
    before, after = jnp.where(odd_z, near, far), jnp.where(odd_z, far, near)
    rec_ext = jnp.concatenate([before[0:1], rec, after[0:1]], axis=0)
    cot_ext = jnp.concatenate([before[1:3], cot, after[1:3]], axis=0)
    even_x = lax.axis_index("xy") % 2 == 0
    side = (low_lanes((8, 128)) == even_x).astype(jnp.int32)
    rec_far, rec_near = swaps(rec_ext, rec_ext, "xy")
    lift_own, seen_own, part_own, w2 = call(
        own_kernel,
        [((KZ, 2, Y, 128), F32), ((KZ, 2, Y, 128), F32), ((3, 136, Y, 256), F32), ((384, 768), BF)],
        [((3, 256, 384), BF), ((1088, 384), BF)],
    )(rec_ext, spread, u, conv_one, conv_two)
    act, delta, dec, pre, lifted, keep, mask = call(
        forward_kernel,
        [
            ((134, Y, 256), BF), ((132, Y, 128), BF), ((132, Y, 128), BF),
            ((134, Y, 256), F32), ((136, Y, 256), BF), ((132, Y, 128), BF),
            ((136, Y, 256), F32),
        ],
        [
            ((2, KZ, 2, Y, 128), F32), ((2, KZ, 2, Y, 128), F32),
            ((1088, 768), BF), ((3, 136, Y, 256), F32), ((1072, 768), BF), ((134, Y, 384), F32),
        ],
    )(rec_far, rec_near, side, cot_ext, lift_own, seen_own, part_own, u, w1x, w2, spread)
    delta_far, delta_near = swaps(delta, delta, "xy")
    two, hot, part_back, lifted_col, dec, b1x, b0, ud, pick, parent, slope = call(
        second_grad_kernel,
        [
            ((27, 32, 128), BF), ((1024, 512), BF), ((3, 132, Y, 256), F32), ((1056, 768), BF),
            ((Z, Y, 128), BF), ((3, 768, 256), BF), ((768, 384), BF), ((2, 128, 128), BF),
            ((256, 512), BF), ((512, 128), BF), ((134, Y, 256), F32),
        ],
        [
            ((3, 384, 256), BF), ((136, Y, 128), F32), ((384, 1072), BF), ((1072, 768), BF), ((384, 768), F32),
            ((1056, 384), BF), ((DEV * ROWS, 128), F32),
        ],
        home=(False, False, False, False, True, *[False] * 6),
    )(act, delta, recv, lifted, dec, rec, pre, mask, *weights)
    decoded = dec.reshape(Z, Y, 2, C).transpose(3, 2, 1, 0)
    message = call(
        backward_kernel,
        ((DEV, 24, 128), BF),
        [
            ((1056, 768), BF), ((3, 132, Y, 256), F32), ((1040, 768), BF), ((130, Y, 384), F32),
            ((134, Y, 128), F32), ((384, 1056), BF), ((384, 768), F32), ((K, 2, Y, 128), F32),
        ],
    )(
        delta_far, delta_near, side, slope, keep, hot, part_back, lifted_col, two, b1x, b0, ud, pick, parent
    )
    back = exchange(message)
    total = call(functools.partial(sum_kernel, scale=scale), ((DEV, 16, 128), BF))(back)
    gathered = exchange(total)
    grad_parent = call(slot_kernel, ((1, C, 2048), BF), home=True)(back)
    grad_one, grad_two, grad_up = call(
        unpack_kernel, [((27, C, C), F32), ((27, C, C), F32), ((8, C, C), F32)], home=True
    )(gathered)
    return decoded, grad_parent, grad_one, grad_two, grad_up


def solution(mesh):
    placed = (
        P(("gz", "xy"), None, None),
        P(("gz", "xy"), None),
        P(("gz", "xy"), None),
        P(),
        P(),
        P(),
        P("xy", None, "gz"),
        P(None, "xy", None, "gz"),
    )
    return jax.shard_map(
        local,
        mesh=mesh,
        in_specs=placed,
        out_specs=(P(None, "xy", None, "gz"), P(("gz", "xy"), None, None), P(), P(), P()),
        check_vma=False,
    )
```
